32 devices in a mesh: groups: 2 (over x), qrow: 4 (over y, core), kcol: 4 (over z).
Axes of the slice: x: 2, y: 2, z: 4, core: 2. Of those that a mesh axis runs over, the one named last changes fastest.
Arguments:
- queries: bfloat16 [8192, 512], P(('groups', 'qrow', 'kcol')), parts along dimension 0, may hold values from -6 to 6
- keys: bfloat16 [8192, 128], P(('groups', 'kcol', 'qrow')), parts along dimension 0, may hold values from -6 to 6
- values: bfloat16 [8192, 128], P(('groups', 'kcol', 'qrow')), parts along dimension 0, may hold values from -6 to 6
- out_grad: bfloat16 [8192, 512], P(('groups', 'qrow', 'kcol')), parts along dimension 0, may hold values from -6 to 6
- pattern: int32 [64, 10], P('groups'), parts along dimension 0, may hold values from 0 to 31, as said below
Outputs:
- attended: bfloat16 [8192, 512], P(('groups', 'qrow', 'kcol')), parts along dimension 0
- query_grad: bfloat16 [8192, 512], P(('groups', 'qrow', 'kcol')), parts along dimension 0
- key_grad: bfloat16 [8192, 128], P(('groups', 'kcol', 'qrow')), parts along dimension 0
- value_grad: bfloat16 [8192, 128], P(('groups', 'kcol', 'qrow')), parts along dimension 0
The draws below stay inside these ranges and needn't reach their ends.
There are 2 independent parts, one for each index of `groups`. The reference program is written for one: setup_inputs(seed, part) draws one part's arguments, and reference() takes and returns one part's arrays. A program takes and returns all parts, laid end to end along the dimension named above; each array names one. Nothing has to cross between parts.
Inputs may be any that keep to these rules, and one draw needn't show every extreme that they name: `pattern`: each row lists distinct key blocks, block b among them. Counting key blocks in aligned groups of 8, a row has at least one entry in every group, at most 4 in one group, and exactly 4 in the group that holds b.
All inputs are finite; a program needn't handle non-finite values.
Results may differ from the reference program's by a relative error of at most 0.038.
Values may be sent and summed in bfloat16 or wider, within the bound.
A program may use at most 128 MiB of HBM per device.

```python
import jax
import jax.numpy as jnp
from jax import lax

H = 4
HD = 128
BLK = 128
OTH = 2
TOKENS = 4096
NB = 32
KB = 8
CAP = 4
NNZ = 10


def background(key, shape):
    return jax.random.truncated_normal(key, -6.0, 6.0, shape)


def draw_queries(key, part):
    field = background(jax.random.fold_in(key, 1), (NB, BLK, H, HD))
    return field.reshape(TOKENS, H * HD).astype(jnp.bfloat16)


def draw_keys(key, part):
    field = background(jax.random.fold_in(key, 2), (NB, BLK, HD))
    return field.reshape(TOKENS, HD).astype(jnp.bfloat16)


def draw_pattern(key, part):
    row_ids = jnp.arange(NB, dtype=jnp.int32)
    home_group = row_ids // KB
    offset_in = row_ids % KB
    nearby = home_group[:, None] * KB + (offset_in[:, None] + jnp.arange(CAP, dtype=jnp.int32)[None, :] - CAP // 2) % KB
    spacing = KB // OTH
    pieces = [nearby]
    group_count = (NNZ - CAP) // OTH + 1
    for shift_by in range(1, group_count):
        target = (home_group + shift_by) % group_count
        phases = jax.random.randint(jax.random.fold_in(key, shift_by), (NB,), 0, spacing)
        spots = (offset_in[:, None] + phases[:, None] + jnp.arange(OTH, dtype=jnp.int32)[None, :] * spacing) % KB
        pieces.append(target[:, None] * KB + spots)
    listing = jnp.concatenate(pieces, axis=1)
    ranking = jax.random.randint(jax.random.fold_in(key, 999), (NB, NNZ), 0, 1000) * NNZ + jnp.arange(NNZ, dtype=jnp.int32)[None, :]
    ordering = jnp.argsort(ranking, axis=1)
    return jnp.take_along_axis(listing, ordering, axis=1).astype(jnp.int32)


def shard_levels(stream_key, extent, cuts, smallest, high):
    factor_of, own = 1.0, jax.random.fold_in(stream_key, 6)
    for axis_at, parts in cuts:
        heights = jnp.exp(jax.random.uniform(jax.random.fold_in(own, axis_at), (parts,), jnp.float32, smallest / len(cuts), high / len(cuts)))
        factor_of = factor_of * jnp.repeat(heights, extent[axis_at] // parts).reshape([-1 if axis == axis_at else 1 for axis in range(len(extent))])
    return factor_of


def normal_values(rng, dims, scale, limit, shards=(), kind=jnp.bfloat16):
    drawn = scale * jax.random.normal(rng, dims, jnp.float32)
    if shards:
        drawn = drawn * shard_levels(rng, dims, shards, -0.22, 0.18)
    return jnp.clip(drawn, -limit, limit).astype(kind)


def setup_inputs(seed: int = 0, part: int = 0) -> dict:
    key_list = jax.random.split(jax.random.key(seed), 6)
    part_splits = jax.random.split(jax.random.fold_in(key_list[5], part), 6)
    return {
        "queries": draw_queries(jax.random.fold_in(jax.random.fold_in(key_list[5], part), 71), part),
        "keys": draw_keys(jax.random.fold_in(jax.random.fold_in(key_list[5], part), 71), part),
        "values": normal_values(part_splits[2], (TOKENS, HD), 1.0, 6.0, ((0, 16),)),
        "out_grad": normal_values(part_splits[3], (TOKENS, H * HD), 1.0, 6.0, ((0, 16),)),
        "pattern": draw_pattern(jax.random.fold_in(jax.random.fold_in(key_list[5], part), 71), part),
    }


def reference(queries, keys, values, out_grad, pattern):
    scaling = HD ** -0.5
    k_tiles = keys.reshape(NB, BLK, HD)
    v_tiles = values.reshape(NB, BLK, HD)
    q_blocks = queries.reshape(NB, BLK, H, HD)
    g_blocks = out_grad.reshape(NB, BLK, H, HD)

    def block_scores(q_block, entries):
        k_slots = k_tiles[entries].reshape(NNZ * BLK, HD).astype(jnp.float32)
        scores = jnp.einsum("thd,sd->hts", q_block.astype(jnp.float32), k_slots) * scaling
        return scores, k_slots

    def forward(packed):
        q_block, g_block, entries = packed
        scores, k_slots = block_scores(q_block, entries)
        v_slots = v_tiles[entries].reshape(NNZ * BLK, HD).astype(jnp.float32)
        row_top = jnp.max(scores, axis=2)
        weights = jnp.exp(scores - row_top[:, :, None])
        totals = jnp.sum(weights, axis=2)
        weights_low = lax.optimization_barrier(weights.astype(jnp.bfloat16)).astype(jnp.float32)
        mixture = jnp.einsum("hts,sd->thd", weights_low, v_slots)
        attended = (mixture / jnp.transpose(totals)[:, :, None]).astype(jnp.bfloat16)
        log_sum = row_top + jnp.log(totals)
        delta = jnp.sum(g_block.astype(jnp.float32) * attended.astype(jnp.float32), axis=2)
        return attended, log_sum, delta

    attended, log_sums, deltas = lax.map(forward, (q_blocks, g_blocks, pattern))

    def backward(carried, packed):
        key_acc, value_acc = carried
        q_block, g_block, entries, log_sum, delta = packed
        scores, k_slots = block_scores(q_block, entries)
        v_slots = v_tiles[entries].reshape(NNZ * BLK, HD).astype(jnp.float32)
        prob_full = jnp.exp(scores - log_sum[:, :, None])
        prob_low = lax.optimization_barrier(prob_full.astype(jnp.bfloat16)).astype(jnp.float32)
        g_float = g_block.astype(jnp.float32)
        grad_prob = jnp.einsum("thd,sd->hts", g_float, v_slots)
        grad_score = prob_full * (grad_prob - jnp.transpose(delta)[:, :, None])
        grad_score = lax.optimization_barrier(grad_score.astype(jnp.bfloat16)).astype(jnp.float32)
        grad_query = jnp.einsum("hts,sd->thd", grad_score, k_slots) * scaling
        grad_key = jnp.einsum("hts,thd->sd", grad_score, q_block.astype(jnp.float32)) * scaling
        grad_value = jnp.einsum("hts,thd->sd", prob_low, g_float)
        key_acc = key_acc.at[entries].add(grad_key.reshape(NNZ, BLK, HD))
        value_acc = value_acc.at[entries].add(grad_value.reshape(NNZ, BLK, HD))
        return (key_acc, value_acc), grad_query.astype(jnp.bfloat16)

    empty_acc = jnp.zeros((NB, BLK, HD), jnp.float32)
    (key_acc, value_acc), grad_queries = lax.scan(
        backward, (empty_acc, empty_acc), (q_blocks, g_blocks, pattern, log_sums, deltas))
    return (attended.reshape(TOKENS, H * HD),
            grad_queries.reshape(TOKENS, H * HD),
            key_acc.reshape(TOKENS, HD).astype(jnp.bfloat16),
            value_acc.reshape(TOKENS, HD).astype(jnp.bfloat16))
```

```python
import functools
import math

import jax
import jax.numpy as jnp
from jax import lax
from jax.experimental import pallas as pl
from jax.experimental.pallas import tpu as pltpu
from jax.sharding import PartitionSpec as P

H = 4
HD = 128
BLK = 128
MESH = pl.DeviceIdType.MESH
F32 = jnp.float32
BF16 = jnp.bfloat16


def dot(a, b):
    return jnp.dot(a, b, preferred_element_type=F32)


def dot_t(a, b):
    return lax.dot_general(a, b, (((0,), (0,)), ((), ())), preferred_element_type=F32)


def kernel(
    nq, nk, nnz, q_ref, g_ref, k_ref, v_ref, pat_ref, o_ref, dq_ref, dk_ref, dv_ref,
    kv, core_in, y_in, z_in, slots, s_scr, qs, gs, qt, gt, kc_scr, vc_scr, inv,
    ag_send, ag_recv, core_send, core_recv, y_send, y_recv, z_send, z_recv,
):
    ny = nq // 2
    qb = q_ref.shape[0] // BLK
    kb = k_ref.shape[0] // BLK
    key_blocks = nq * nk * kb
    chunk = 2 if nnz % 2 == 0 else 1
    scaling = HD ** (-0.5)
    r = lax.axis_index("qrow")
    c = lax.axis_index("kcol")
    y, core = r // 2, r % 2
    other = 1 - core

    def shard(c_at, y_at, core_at):
        return c_at * nq + y_at * 2 + core_at

    def zed(d):
        return (c + d) % nk

    def why(e):
        return (y + e) % ny

    def at(c_to, y_to, core_to):
        return {"qrow": y_to * 2 + core_to, "kcol": c_to}

    def remote(src, dst, send, recv, where):
        return pltpu.make_async_remote_copy(
            src_ref=src, dst_ref=dst, send_sem=send, recv_sem=recv,
            device_id=where, device_id_type=MESH,
        )

    core_peer = at(c, y, other)

    barrier = pltpu.get_barrier_semaphore()
    for d in range(1, nk):
        pl.semaphore_signal(barrier, inc=1, device_id=at(zed(d), y, core), device_id_type=MESH)
    for e in range(1, ny):
        pl.semaphore_signal(barrier, inc=1, device_id=at(c, why(e), core), device_id_type=MESH)
    pl.semaphore_signal(barrier, inc=1, device_id=core_peer, device_id_type=MESH)

    own = shard(c, y, core)
    kv[own, 0] = k_ref[...].reshape(kb, BLK, HD)
    kv[own, 1] = v_ref[...].reshape(kb, BLK, HD)
    pl.semaphore_wait(barrier, nk - 1 + ny - 1 + 1)

    z_sends = nk - 1
    y_sends = nk * (ny - 1)

    def gather(slot, s, where):
        return remote(kv.at[s], kv.at[s], ag_send.at[slot], ag_recv.at[s], where)

    def arrived(s):
        gather(0, s, core_peer).wait_recv()

    for d in range(1, nk):
        gather(d - 1, own, at(zed(d), y, core)).start()
    for e in range(1, ny):
        gather(z_sends + e - 1, own, at(c, why(e), core)).start()
    gather(z_sends + y_sends, own, core_peer).start()

    for b in range(qb):
        for h in range(H):
            q_h = q_ref[b * BLK : (b + 1) * BLK, h * HD : (h + 1) * HD]
            g_h = g_ref[b * BLK : (b + 1) * BLK, h * HD : (h + 1) * HD]
            qs[b, h * BLK : (h + 1) * BLK, :] = q_h
            gs[b, h * BLK : (h + 1) * BLK, :] = g_h
            qt[b, :, h * BLK : (h + 1) * BLK] = q_h.T
            gt[b, :, h * BLK : (h + 1) * BLK] = g_h.T

    zero_slot = qb * nnz
    slots[0, zero_slot] = jnp.zeros((BLK, HD), F32)
    slots[1, zero_slot] = jnp.zeros((BLK, HD), F32)
    first_row = (r * nk + c) * qb

    for d in range(1, nk):
        s = shard(zed(nk - d), y, core)
        arrived(s)
        for e in range(1, ny):
            gather(z_sends + d * (ny - 1) + e - 1, s, at(c, why(e), core)).start()
        gather(z_sends + y_sends + d, s, core_peer).start()

    def invert(j, carry):
        for b in range(qb):
            found = jnp.int32(zero_slot)
            for n in range(nnz):
                found = jnp.where(pat_ref[n, first_row + b] == j, b * nnz + n, found)
            inv[b, j] = found
        return carry

    lax.fori_loop(0, key_blocks, invert, 0)

    def from_y(i, carry):
        e, d = i // nk + 1, i % nk
        s = shard(zed(nk - d), why(ny - e), core)
        arrived(s)
        gather(z_sends + y_sends + nk + i, s, core_peer).start()
        return carry

    lax.fori_loop(0, y_sends, from_y, 0)

    def from_core(i, carry):
        arrived(shard(i % nk, i // nk, other))
        return carry

    lax.fori_loop(0, nk * ny, from_core, 0)

    rows = chunk * BLK
    for b in range(qb):
        for n in range(nnz):
            j = pat_ref[n, first_row + b]
            kc_scr[b, n * BLK : (n + 1) * BLK, :] = kv[j // kb, 0, j % kb]
            vc_scr[b, n * BLK : (n + 1) * BLK, :] = kv[j // kb, 1, j % kb]
    for b in range(qb):
        top = None
        for n in range(0, nnz, chunk):
            part = slice(n * BLK, n * BLK + rows)
            scores = dot(kc_scr[b, part, :], qt[b])
            s_scr[b, part, :] = scores
            high = jnp.max(scores, axis=0, keepdims=True)
            top = high if top is None else jnp.maximum(top, high)
        total = jnp.zeros((1, H * BLK), F32)
        mix = jnp.zeros((HD, H * BLK), F32)
        for n in range(0, nnz, chunk):
            part = slice(n * BLK, n * BLK + rows)
            weights = jnp.exp2((s_scr[b, part, :] - top) * (scaling * math.log2(math.e)))
            s_scr[b, part, :] = weights
            total = total + jnp.sum(weights, axis=0, keepdims=True)
            mix = mix + dot_t(vc_scr[b, part, :], weights.astype(BF16))
        attended = (mix / total).astype(BF16)
        delta = jnp.sum(gt[b].astype(F32) * attended.astype(F32), axis=0, keepdims=True)
        share = 1.0 / total
        for h in range(H):
            o_ref[b * BLK : (b + 1) * BLK, h * HD : (h + 1) * HD] = attended[
                :, h * BLK : (h + 1) * BLK
            ].T
        grad_q = jnp.zeros((HD, H * BLK), F32)
        for n in range(0, nnz, chunk):
            part = slice(n * BLK, n * BLK + rows)
            grad_prob = dot(vc_scr[b, part, :], gt[b])
            prob = s_scr[b, part, :] * share
            grad_score = (prob * (grad_prob - delta)).astype(BF16)
            grad_v = dot(prob.astype(BF16), gs[b])
            grad_k = dot(grad_score, qs[b]) * scaling
            grad_q = grad_q + dot_t(kc_scr[b, part, :], grad_score)
            for i in range(chunk):
                slots[0, b * nnz + n + i] = grad_k[i * BLK : (i + 1) * BLK]
                slots[1, b * nnz + n + i] = grad_v[i * BLK : (i + 1) * BLK]
        grad_q = (grad_q * scaling).astype(BF16)
        for h in range(H):
            dq_ref[b * BLK : (b + 1) * BLK, h * HD : (h + 1) * HD] = grad_q[
                :, h * BLK : (h + 1) * BLK
            ].T

    def gathers_sent(i, carry):
        gather(i, own, core_peer).wait_send()
        return carry

    lax.fori_loop(0, z_sends + y_sends + nk * ny, gathers_sent, 0)

    def partial(s, which, half):
        j = s * kb + half
        value = slots[which, inv[0, j]]
        for b in range(1, qb):
            value = value + slots[which, inv[b, j]]
        return value

    def to_core(i, s):
        return remote(kv.at[s], core_in.at[i], core_send.at[i], core_recv.at[i], core_peer)

    def to_y(i, s, c_at, where, slot):
        return remote(kv.at[s], y_in.at[i], y_send.at[slot], y_recv.at[i], where)

    def to_z(i, s, where):
        return remote(kv.at[s], z_in.at[i], z_send.at[i], z_recv.at[i], where)

    def order(i):
        return zed((i % nk + 1) % nk), why((i // nk + 1) % ny)

    def core_step(i, carry):
        c_at, y_at = order(i)
        s = shard(c_at, y_at, other)
        for which in range(2):
            for half in range(kb):
                kv[s, which, half] = partial(s, which, half).astype(BF16)
        to_core(i, s).start()
        return carry

    lax.fori_loop(0, nk * ny, core_step, 0)

    def y_step(i, carry):
        c_at, y_at = order(i)
        s = shard(c_at, y_at, core)
        to_core(i, s).wait_recv()
        for which in range(2):
            for half in range(kb):
                value = partial(s, which, half) + core_in[i, which, half].astype(F32)
                kv[s, which, half] = value.astype(BF16)
        to_y(i, s, c_at, at(c, y_at, core), i).start()
        return carry

    lax.fori_loop(0, y_sends, y_step, 0)

    def summed(d, s, which, half):
        i = y_sends + (d + nk - 1) % nk
        value = partial(s, which, half) + core_in[i, which, half].astype(F32)
        for e in range(1, ny):
            value = value + y_in[(e - 1) * nk + (d + nk - 1) % nk, which, half].astype(F32)
        return value

    def landed(d, s):
        to_core(y_sends + (d + nk - 1) % nk, s).wait_recv()
        for e in range(1, ny):
            to_y((e - 1) * nk + (d + nk - 1) % nk, s, c, core_peer, 0).wait_recv()

    for d in range(1, nk):
        s = shard(zed(d), y, core)
        landed(d, s)
        for which in range(2):
            for half in range(kb):
                kv[s, which, half] = summed(d, s, which, half).astype(BF16)
        to_z(d - 1, s, at(zed(d), y, core)).start()
    landed(0, own)
    for d in range(1, nk):
        to_z(d - 1, own, core_peer).wait_recv()
    for which, out in ((0, dk_ref), (1, dv_ref)):
        for half in range(kb):
            value = summed(0, own, which, half)
            for d in range(1, nk):
                value = value + z_in[d - 1, which, half].astype(F32)
            out[half * BLK : (half + 1) * BLK, :] = value.astype(BF16)

    def core_sent(i, carry):
        to_core(i, own).wait_send()
        return carry

    def y_sent(i, carry):
        to_y(0, own, c, core_peer, i).wait_send()
        return carry

    lax.fori_loop(0, nk * ny, core_sent, 0)
    lax.fori_loop(0, y_sends, y_sent, 0)
    for d in range(1, nk):
        to_z(d - 1, own, core_peer).wait_send()


def write_out(*refs):
    half = len(refs) // 2
    sem = refs[-1]
    copies = [
        pltpu.make_async_copy(src, dst, sem.at[i])
        for i, (src, dst) in enumerate(zip(refs[:half], refs[half:-1]))
    ]
    for copy in copies:
        copy.start()
    for copy in copies:
        copy.wait()


def to_hbm(results):
    n = len(results)
    return pl.pallas_call(
        write_out,
        out_shape=tuple(jax.ShapeDtypeStruct(a.shape, a.dtype) for a in results),
        in_specs=[pl.BlockSpec(memory_space=pltpu.VMEM)] * n,
        out_specs=(pl.BlockSpec(memory_space=pl.ANY),) * n,
        scratch_shapes=[pltpu.SemaphoreType.DMA((n,))],
        compiler_params=pltpu.CompilerParams(vmem_limit_bytes=4 * 1024 * 1024),
    )(*results)


def body(nq, nk, queries, keys, values, out_grad, pattern):
    pattern = pattern.T
    nnz = pattern.shape[0]
    ny = nq // 2
    qb = queries.shape[0] // BLK
    kb = keys.shape[0] // BLK
    shards = nq * nk
    block = (2, kb, BLK, HD)
    y_sends = nk * (ny - 1)
    dma = pltpu.SemaphoreType.DMA
    vmem = pl.BlockSpec(memory_space=pltpu.VMEM)
    results = pl.pallas_call(
        functools.partial(kernel, nq, nk, nnz),
        out_shape=(
            pltpu.VMEM(queries.shape, BF16),
            pltpu.VMEM(queries.shape, BF16),
            pltpu.VMEM(keys.shape, BF16),
            pltpu.VMEM(keys.shape, BF16),
        ),
        in_specs=[vmem] * 4 + [pl.BlockSpec(memory_space=pltpu.SMEM)],
        out_specs=(vmem,) * 4,
        scratch_shapes=[
            pltpu.VMEM((shards,) + block, BF16),
            pltpu.VMEM((nk * ny,) + block, BF16),
            pltpu.VMEM((max(y_sends, 1),) + block, BF16),
            pltpu.VMEM((max(nk - 1, 1),) + block, BF16),
            pltpu.VMEM((2, qb * nnz + 1, BLK, HD), F32),
            pltpu.VMEM((qb, nnz * BLK, H * BLK), F32),
            pltpu.VMEM((qb, H * BLK, HD), BF16),
            pltpu.VMEM((qb, H * BLK, HD), BF16),
            pltpu.VMEM((qb, HD, H * BLK), BF16),
            pltpu.VMEM((qb, HD, H * BLK), BF16),
            pltpu.VMEM((qb, nnz * BLK, HD), BF16),
            pltpu.VMEM((qb, nnz * BLK, HD), BF16),
            pltpu.SMEM((qb, shards * kb), jnp.int32),
            dma((nk - 1 + y_sends + nk * ny,)),
            dma((shards,)),
            dma((nk * ny,)),
            dma((nk * ny,)),
            dma((max(y_sends, 1),)),
            dma((max(y_sends, 1),)),
            dma((max(nk - 1, 1),)),
            dma((max(nk - 1, 1),)),
        ],
        compiler_params=pltpu.CompilerParams(
            collective_id=0, has_side_effects=True, vmem_limit_bytes=58 * 1024 * 1024
        ),
    )(queries, out_grad, keys, values, pattern)
    return to_hbm(results)


def solution(mesh):
    return jax.shard_map(
        functools.partial(body, mesh.shape["qrow"], mesh.shape["kcol"]),
        mesh=mesh,
        in_specs=(
            P(("groups", "qrow", "kcol"), None),
            P(("groups", "kcol", "qrow"), None),
            P(("groups", "kcol", "qrow"), None),
            P(("groups", "qrow", "kcol"), None),
            P("groups", None),
        ),
        out_specs=(
            P(("groups", "qrow", "kcol"), None),
            P(("groups", "qrow", "kcol"), None),
            P(("groups", "kcol", "qrow"), None),
            P(("groups", "kcol", "qrow"), None),
        ),
        check_vma=False,
    )
```

```python
import functools
import math

import jax
import jax.numpy as jnp
from jax import lax
from jax.experimental import pallas as pl
from jax.experimental.pallas import tpu as pltpu
from jax.sharding import PartitionSpec as P

H = 4
HD = 128
BLK = 128
MESH = pl.DeviceIdType.MESH
F32 = jnp.float32
BF16 = jnp.bfloat16


def dot(a, b):
    return jnp.dot(a, b, preferred_element_type=F32)


def dot_t(a, b):
    return lax.dot_general(a, b, (((0,), (0,)), ((), ())), preferred_element_type=F32)


def kernel(
    nq, nk, nnz, q_hbm, g_hbm, k_hbm, v_hbm, pat_ref, o_ref, dq_ref, dk_ref, dv_ref,
    q_ref, g_ref, kbuf, vbuf, vout, core_in, y_in, z_in, kslots, vslots, s_scr, share_scr,
    qs, gs, qt, gt, kc_scr, vc_scr, inv,
    in_sem, gz_send, gz_recv, gy_send, gy_recv, gc_send, gc_recv,
    core_send, core_recv, y_send, y_recv, z_send, z_recv,
):
    ny = nq // 2
    qb = q_ref.shape[0] // BLK
    kb = kbuf.shape[1]
    key_blocks = nq * nk * kb
    chunk = 2 if nnz % 2 == 0 else 1
    rows = chunk * BLK
    scaling = HD ** (-0.5)
    bufs = (kbuf, vbuf)
    tight = vout.shape[0] < kbuf.shape[0]
    outs = (vbuf, kbuf) if tight else (kbuf, vout)
    slots = (kslots, vslots)
    r = lax.axis_index("qrow")
    c = lax.axis_index("kcol")
    y, core = r // 2, r % 2
    other = 1 - core

    def loop(n, step):
        if n <= 8:
            for i in range(n):
                step(i)
        else:
            lax.fori_loop(0, n, lambda i, carry: (step(i), carry)[1], 0)

    def shard(c_at, y_at, core_at):
        return c_at * nq + y_at * 2 + core_at

    def zed(d):
        return (c + d) % nk

    def why(e):
        return (y + e) % ny

    def at(c_to, y_to, core_to):
        return {"qrow": y_to * 2 + core_to, "kcol": c_to}

    low_half = 1 - (2 * c) // nk

    def far(k):
        up, down = k, nk - 1 - k
        up = up + (nk + up - c) // nk
        down = down - (nk + c - down) // nk
        picked = low_half * down + (1 - low_half) * up
        last = k // (nk - 1) if nk > 1 else 1
        return last * c + (1 - last) * picked

    def remote(src, dst, send, recv, where):
        return pltpu.make_async_remote_copy(
            src_ref=src, dst_ref=dst, send_sem=send, recv_sem=recv,
            device_id=where, device_id_type=MESH,
        )

    core_peer = at(c, y, other)
    own = shard(c, y, core)

    barrier = pltpu.get_barrier_semaphore()
    for d in range(1, nk):
        pl.semaphore_signal(barrier, inc=1, device_id=at(zed(d), y, core), device_id_type=MESH)
    for e in range(1, ny):
        pl.semaphore_signal(barrier, inc=1, device_id=at(c, why(e), core), device_id_type=MESH)
    pl.semaphore_signal(barrier, inc=1, device_id=core_peer, device_id_type=MESH)

    staged = []
    for w, src in ((0, k_hbm), (1, v_hbm)):
        for h in range(kb):
            staged.append(
                pltpu.make_async_copy(
                    src.at[pl.ds(h * BLK, BLK)], bufs[w].at[own, h], in_sem.at[w * kb + h]
                )
            )
    staged.append(pltpu.make_async_copy(q_hbm, q_ref, in_sem.at[2 * kb]))
    staged.append(pltpu.make_async_copy(g_hbm, g_ref, in_sem.at[2 * kb + 1]))
    for copy in staged:
        copy.start()
    for copy in staged[: 2 * kb]:
        copy.wait()
    pl.semaphore_wait(barrier, nk - 1 + ny - 1 + 1)

    def send_z(w, src_c, h, way):
        s = shard(src_c, y, core)
        return remote(
            bufs[w].at[s, h], bufs[w].at[s, h],
            gz_send.at[w, (way + 1) // 2, src_c], gz_recv.at[w, src_c, h], at(c + way, y, core),
        )

    def send_y(w, src_c, h, e):
        s = shard(src_c, y, core)
        return remote(
            bufs[w].at[s, h], bufs[w].at[s, h],
            gy_send.at[w], gy_recv.at[w, e - 1, src_c], at(c, why(e), core),
        )

    def send_core(w, s):
        return remote(bufs[w].at[s], bufs[w].at[s], gc_send.at[w], gc_recv.at[w], core_peer)

    def spread(w, src_c, h, ways):
        for way in ways:
            @pl.when((c + way >= 0) & (c + way < nk))
            def _():
                send_z(w, src_c, h, way).start()
        loop(ny - 1, lambda e: send_y(w, src_c, h, e + 1).start())

    def forward(w, d):
        for side in (-1, 1):
            src_c = c + side * d

            @pl.when((src_c >= 0) & (src_c < nk))
            def _():
                for h in range(kb):
                    send_z(w, src_c, h, -side).wait_recv()
                    spread(w, src_c, h, (-side,))
                send_core(w, shard(src_c, y, core)).start()

    def from_y(w, first, last):
        for m in range(first, last):
            src_c = far(nk - 1 - m)

            def arrived(e):
                s = shard(src_c, why(ny - 1 - e), core)
                remote(
                    bufs[w].at[s], bufs[w].at[s], gy_send.at[w], gy_recv.at[w, e, src_c], core_peer
                ).wait_recv()
                send_core(w, s).start()

            loop(ny - 1, arrived)

    def from_core(w):
        every = bufs[w].at[pl.ds(0, nk * ny)]
        remote(every, every, gc_send.at[w], gc_recv.at[w], core_peer).wait_recv()

    def gather_sent(w):
        every = bufs[w].at[pl.ds(0, nk * ny)]
        remote(every, every, gc_send.at[w], gc_recv.at[w], core_peer).wait_send()
        if ny > 1:
            part = bufs[w].at[pl.ds(0, nk * (ny - 1))]
            remote(part, part, gy_send.at[w], gc_recv.at[w], core_peer).wait_send()
        one = bufs[w].at[0]
        for src_c in range(nk):
            @pl.when((c >= src_c) & (c + 1 < nk))
            def _():
                remote(one, one, gz_send.at[w, 1, src_c], gc_recv.at[w], core_peer).wait_send()

            @pl.when((c <= src_c) & (c >= 1))
            def _():
                remote(one, one, gz_send.at[w, 0, src_c], gc_recv.at[w], core_peer).wait_send()

    for h in range(kb):
        spread(0, c, h, (-1, 1))
    spread(1, c, 0, (-1, 1))
    send_core(0, own).start()

    for copy in staged[2 * kb :]:
        copy.wait()
    for b in range(qb):
        for h in range(H):
            q_h = q_ref[b * BLK : (b + 1) * BLK, h * HD : (h + 1) * HD]
            g_h = g_ref[b * BLK : (b + 1) * BLK, h * HD : (h + 1) * HD]
            qs[b, h * BLK : (h + 1) * BLK, :] = q_h
            gs[b, h * BLK : (h + 1) * BLK, :] = g_h
            qt[b, :, h * BLK : (h + 1) * BLK] = q_h.T
            gt[b, :, h * BLK : (h + 1) * BLK] = g_h.T

    zero_slot = qb * nnz
    kslots[zero_slot] = jnp.zeros((BLK, HD), F32)
    vslots[zero_slot] = jnp.zeros((BLK, HD), F32)
    first_row = (r * nk + c) * qb

    if nk > 1:
        forward(0, 1)
    for h in range(1, kb):
        spread(1, c, h, (-1, 1))
    send_core(1, own).start()

    def invert(j, carry):
        for b in range(qb):
            found = jnp.int32(zero_slot)
            for n in range(nnz):
                found = jnp.where(pat_ref[n, first_row + b] == j, b * nnz + n, found)
            inv[b, j] = found
        return carry

    for d in range(2, nk):
        forward(0, d)
        forward(1, d - 1)
        if d == 2:
            lax.fori_loop(0, key_blocks, invert, 0)
    if nk < 3:
        lax.fori_loop(0, key_blocks, invert, 0)
    from_y(0, 0, nk - 1)
    if nk > 1:
        forward(1, nk - 1)
    from_y(0, nk - 1, nk)
    from_core(0)

    def partial(w, s, half):
        j = s * kb + half
        value = slots[w][inv[0, j]]
        for b in range(1, qb):
            value = value + slots[w][inv[b, j]]
        return value

    def to_core(w, i, s):
        return remote(outs[w].at[s], core_in.at[w, i], core_send.at[w], core_recv.at[w, i], core_peer)

    def to_y(w, i, s, where):
        return remote(outs[w].at[s], y_in.at[w, i], y_send.at[w], y_recv.at[w, i], where)

    def to_z(w, s, where):
        return remote(outs[w].at[s], z_in.at[w, c], z_send.at[w], z_recv.at[w], where)

    def place(i):
        return far(i % nk), why((i // nk + 1) % ny)

    y_sends = nk * (ny - 1)

    def core_step(w):
        def step(i):
            c_at, y_at = place(i)
            s = shard(c_at, y_at, other)
            for half in range(kb):
                outs[w][s, half] = partial(w, s, half).astype(BF16)
            to_core(w, i, s).start()

        loop(nk * ny, step)

    def y_step(w):
        def step(i):
            c_at, y_at = place(i)
            s = shard(c_at, y_at, core)
            to_core(w, i, s).wait_recv()
            for half in range(kb):
                value = partial(w, s, half) + core_in[w, i, half].astype(F32)
                outs[w][s, half] = value.astype(BF16)
            to_y(w, i, s, at(c, y_at, core)).start()

        loop(y_sends, step)

    def summed(w, k, s, half):
        value = partial(w, s, half) + core_in[w, y_sends + k, half].astype(F32)
        for e in range(1, ny):
            value = value + y_in[w, (e - 1) * nk + k, half].astype(F32)
        return value

    def landed(w, k, s):
        to_core(w, y_sends + k, s).wait_recv()
        for e in range(1, ny):
            to_y(w, (e - 1) * nk + k, s, core_peer).wait_recv()

    def z_step(w, k):
        c_at = far(k)
        s = shard(c_at, y, core)
        landed(w, k, s)
        for half in range(kb):
            outs[w][s, half] = summed(w, k, s, half).astype(BF16)
        to_z(w, s, at(c_at, y, core)).start()

    def finish(w, out):
        landed(w, nk - 1, own)
        if nk > 1:
            some = z_in.at[w, pl.ds(0, nk - 1)]
            remote(some, some, z_send.at[w], z_recv.at[w], core_peer).wait_recv()
        for half in range(kb):
            value = summed(w, nk - 1, own, half)
            for d in range(1, nk):
                value = value + z_in[w, zed(d), half].astype(F32)
            out[half * BLK : (half + 1) * BLK, :] = value.astype(BF16)

    def reduction_sent(w):
        every = outs[w].at[pl.ds(0, nk * ny)]
        remote(every, every, core_send.at[w], z_recv.at[w], core_peer).wait_send()
        if ny > 1:
            part = outs[w].at[pl.ds(0, y_sends)]
            remote(part, part, y_send.at[w], z_recv.at[w], core_peer).wait_send()
        if nk > 1:
            part = outs[w].at[pl.ds(0, nk - 1)]
            remote(part, part, z_send.at[w], z_recv.at[w], core_peer).wait_send()

    for b in range(qb):
        for n in range(nnz):
            j = pat_ref[n, first_row + b]
            kc_scr[b, n * BLK : (n + 1) * BLK, :] = kbuf[j // kb, j % kb]
        top = None
        for n in range(0, nnz, chunk):
            part = slice(n * BLK, n * BLK + rows)
            scores = dot(kc_scr[b, part, :], qt[b])
            s_scr[b, part, :] = scores
            high = jnp.max(scores, axis=0, keepdims=True)
            top = high if top is None else jnp.maximum(top, high)
        total = jnp.zeros((1, H * BLK), F32)
        for n in range(0, nnz, chunk):
            part = slice(n * BLK, n * BLK + rows)
            weights = jnp.exp2((s_scr[b, part, :] - top) * (scaling * math.log2(math.e)))
            s_scr[b, part, :] = weights
            total = total + jnp.sum(weights, axis=0, keepdims=True)
        share = 1.0 / total
        share_scr[b, 0:1, :] = share
        share_scr[b, 1:2, :] = total
        for n in range(0, nnz, chunk):
            part = slice(n * BLK, n * BLK + rows)
            grad_v = dot((s_scr[b, part, :] * share).astype(BF16), gs[b])
            for i in range(chunk):
                vslots[b * nnz + n + i] = grad_v[i * BLK : (i + 1) * BLK]

    if tight:
        gather_sent(0)
    core_step(1)
    from_y(1, 0, nk)
    y_step(1)
    if not tight:
        gather_sent(0)
    from_core(1)

    for b in range(qb):
        for n in range(nnz):
            j = pat_ref[n, first_row + b]
            vc_scr[b, n * BLK : (n + 1) * BLK, :] = vbuf[j // kb, j % kb]
        mix = jnp.zeros((HD, H * BLK), F32)
        for n in range(0, nnz, chunk):
            part = slice(n * BLK, n * BLK + rows)
            mix = mix + dot_t(vc_scr[b, part, :], s_scr[b, part, :].astype(BF16))
        share = share_scr[b, 0:1, :]
        attended = (mix / share_scr[b, 1:2, :]).astype(BF16)
        delta = jnp.sum(gt[b].astype(F32) * attended.astype(F32), axis=0, keepdims=True)
        for h in range(H):
            o_ref[b * BLK : (b + 1) * BLK, h * HD : (h + 1) * HD] = attended[
                :, h * BLK : (h + 1) * BLK
            ].T
        grad_q = jnp.zeros((HD, H * BLK), F32)
        for n in range(0, nnz, chunk):
            part = slice(n * BLK, n * BLK + rows)
            grad_prob = dot(vc_scr[b, part, :], gt[b])
            prob = s_scr[b, part, :] * share
            grad_score = (prob * (grad_prob - delta)).astype(BF16)
            grad_k = dot(grad_score, qs[b]) * scaling
            grad_q = grad_q + dot_t(kc_scr[b, part, :], grad_score)
            for i in range(chunk):
                kslots[b * nnz + n + i] = grad_k[i * BLK : (i + 1) * BLK]
        grad_q = (grad_q * scaling).astype(BF16)
        for h in range(H):
            dq_ref[b * BLK : (b + 1) * BLK, h * HD : (h + 1) * HD] = grad_q[
                :, h * BLK : (h + 1) * BLK
            ].T

    if tight:
        gather_sent(1)
    core_step(0)
    if nk > 1:
        z_step(1, 0)
    y_step(0)
    for k in range(1, nk - 1):
        z_step(1, k)
    if not tight:
        gather_sent(1)
    if nk > 1:
        z_step(0, 0)
    finish(1, dv_ref)
    for k in range(1, nk - 1):
        z_step(0, k)
    reduction_sent(1)
    finish(0, dk_ref)
    reduction_sent(0)


def write_out(*refs):
    half = len(refs) // 2
    sem = refs[-1]
    copies = [
        pltpu.make_async_copy(src, dst, sem.at[i])
        for i, (src, dst) in enumerate(zip(refs[:half], refs[half:-1]))
    ]
    for copy in copies:
        copy.start()
    for copy in copies:
        copy.wait()


def to_hbm(results):
    n = len(results)
    return pl.pallas_call(
        write_out,
        out_shape=tuple(jax.ShapeDtypeStruct(a.shape, a.dtype) for a in results),
        in_specs=[pl.BlockSpec(memory_space=pltpu.VMEM)] * n,
        out_specs=(pl.BlockSpec(memory_space=pl.ANY),) * n,
        scratch_shapes=[pltpu.SemaphoreType.DMA((n,))],
        compiler_params=pltpu.CompilerParams(vmem_limit_bytes=4 * 1024 * 1024),
    )(*results)


def body(nq, nk, queries, keys, values, out_grad, pattern):
    pattern = pattern.T
    nnz = pattern.shape[0]
    ny = nq // 2
    qb = queries.shape[0] // BLK
    kb = keys.shape[0] // BLK
    shards = nq * nk
    block = (kb, BLK, HD)
    y_sends = max(nk * (ny - 1), 1)
    dma = pltpu.SemaphoreType.DMA
    vmem = pl.BlockSpec(memory_space=pltpu.VMEM)
    results = pl.pallas_call(
        functools.partial(kernel, nq, nk, nnz),
        out_shape=(
            pltpu.VMEM(queries.shape, BF16),
            pltpu.VMEM(queries.shape, BF16),
            pltpu.VMEM(keys.shape, BF16),
            pltpu.VMEM(keys.shape, BF16),
        ),
        in_specs=[pl.BlockSpec(memory_space=pl.ANY)] * 4 + [pl.BlockSpec(memory_space=pltpu.SMEM)],
        out_specs=(vmem,) * 4,
        scratch_shapes=[
            pltpu.VMEM(queries.shape, BF16),
            pltpu.VMEM(queries.shape, BF16),
            pltpu.VMEM((shards,) + block, BF16),
            pltpu.VMEM((shards,) + block, BF16),
            pltpu.VMEM((shards if shards <= 64 else 1,) + block, BF16),
            pltpu.VMEM((2, nk * ny) + block, BF16),
            pltpu.VMEM((2, y_sends) + block, BF16),
            pltpu.VMEM((2, nk) + block, BF16),
            pltpu.VMEM((qb * nnz + 1, BLK, HD), F32),
            pltpu.VMEM((qb * nnz + 1, BLK, HD), F32),
            pltpu.VMEM((qb, nnz * BLK, H * BLK), F32),
            pltpu.VMEM((qb, 8, H * BLK), F32),
            pltpu.VMEM((qb, H * BLK, HD), BF16),
            pltpu.VMEM((qb, H * BLK, HD), BF16),
            pltpu.VMEM((qb, HD, H * BLK), BF16),
            pltpu.VMEM((qb, HD, H * BLK), BF16),
            pltpu.VMEM((qb, nnz * BLK, HD), BF16),
            pltpu.VMEM((qb, nnz * BLK, HD), BF16),
            pltpu.SMEM((qb, shards * kb), jnp.int32),
            dma((2 * kb + 2,)),
            dma((2, 2, nk)),
            dma((2, nk, kb)),
            dma((2,)),
            dma((2, max(ny - 1, 1), nk)),
            dma((2,)),
            dma((2,)),
            dma((2,)),
            dma((2, nk * ny)),
            dma((2,)),
            dma((2, y_sends)),
            dma((2,)),
            dma((2,)),
        ],
        compiler_params=pltpu.CompilerParams(
            collective_id=0, has_side_effects=True, vmem_limit_bytes=60 * 1024 * 1024
        ),
    )(queries, out_grad, keys, values, pattern)
    return to_hbm(results)


def solution(mesh):
    return jax.shard_map(
        functools.partial(body, mesh.shape["qrow"], mesh.shape["kcol"]),
        mesh=mesh,
        in_specs=(
            P(("groups", "qrow", "kcol"), None),
            P(("groups", "kcol", "qrow"), None),
            P(("groups", "kcol", "qrow"), None),
            P(("groups", "qrow", "kcol"), None),
            P("groups", None),
        ),
        out_specs=(
            P(("groups", "qrow", "kcol"), None),
            P(("groups", "qrow", "kcol"), None),
            P(("groups", "kcol", "qrow"), None),
            P(("groups", "kcol", "qrow"), None),
        ),
        check_vma=False,
    )
```

```python
import functools
import math

import jax
import jax.numpy as jnp
from jax import lax
from jax.experimental import pallas as pl
from jax.experimental.pallas import tpu as pltpu
from jax.sharding import PartitionSpec as P

H = 4
HD = 128
BLK = 128
MESH = pl.DeviceIdType.MESH
F32 = jnp.float32
BF16 = jnp.bfloat16


def dot(a, b):
    return jnp.dot(a, b, preferred_element_type=F32)


def dot_t(a, b):
    return lax.dot_general(a, b, (((0,), (0,)), ((), ())), preferred_element_type=F32)


def kernel(
    nq, nk, nnz, q_hbm, g_hbm, k_hbm, v_hbm, pat_ref, o_ref, dq_ref, dk_ref, dv_ref,
    q_ref, g_ref, kbuf, vbuf, vout, core_in, y_in, z_in, kslots, vslots, s_scr, share_scr,
    qs, gs, qt, gt, kc_scr, vc_scr, att_scr, ds_scr, inv,
    in_sem, gz_send, gz_recv, gy_send, gy_recv, gc_send, gc_recv,
    core_send, core_recv, y_send, y_recv, z_send, z_recv,
):
    ny = nq // 2
    qb = q_ref.shape[0] // BLK
    kb = kbuf.shape[1]
    key_blocks = nq * nk * kb
    chunk = 2 if nnz % 2 == 0 else 1
    rows = chunk * BLK
    scaling = HD ** (-0.5)
    bufs = (kbuf, vbuf)
    tight = vout.shape[0] < kbuf.shape[0]
    outs = (vbuf, kbuf) if tight else (kbuf, vout)
    slots = (kslots, vslots)
    r = lax.axis_index("qrow")
    c = lax.axis_index("kcol")
    y, core = r // 2, r % 2
    other = 1 - core

    def loop(n, step):
        if n <= 8:
            for i in range(n):
                step(i)
        else:
            lax.fori_loop(0, n, lambda i, carry: (step(i), carry)[1], 0)

    def shard(c_at, y_at, core_at):
        return c_at * nq + y_at * 2 + core_at

    def zed(d):
        return (c + d) % nk

    def why(e):
        return (y + e) % ny

    def at(c_to, y_to, core_to):
        return {"qrow": y_to * 2 + core_to, "kcol": c_to}

    low_half = 1 - (2 * c) // nk

    def far(k):
        up, down = k, nk - 1 - k
        up = up + (nk + up - c) // nk
        down = down - (nk + c - down) // nk
        picked = low_half * down + (1 - low_half) * up
        last = k // (nk - 1) if nk > 1 else 1
        return last * c + (1 - last) * picked

    def remote(src, dst, send, recv, where):
        return pltpu.make_async_remote_copy(
            src_ref=src, dst_ref=dst, send_sem=send, recv_sem=recv,
            device_id=where, device_id_type=MESH,
        )

    core_peer = at(c, y, other)
    own = shard(c, y, core)

    barrier = pltpu.get_barrier_semaphore()
    for d in range(1, nk):
        pl.semaphore_signal(barrier, inc=1, device_id=at(zed(d), y, core), device_id_type=MESH)
    for e in range(1, ny):
        pl.semaphore_signal(barrier, inc=1, device_id=at(c, why(e), core), device_id_type=MESH)
    pl.semaphore_signal(barrier, inc=1, device_id=core_peer, device_id_type=MESH)

    staged = []
    for w, src in ((0, k_hbm), (1, v_hbm)):
        for h in range(kb):
            staged.append(
                pltpu.make_async_copy(
                    src.at[pl.ds(h * BLK, BLK)], bufs[w].at[own, h], in_sem.at[w * kb + h]
                )
            )
    staged.append(pltpu.make_async_copy(q_hbm, q_ref, in_sem.at[2 * kb]))
    staged.append(pltpu.make_async_copy(g_hbm, g_ref, in_sem.at[2 * kb + 1]))
    for copy in staged:
        copy.start()
    for copy in staged[: 2 * kb]:
        copy.wait()
    pl.semaphore_wait(barrier, nk - 1 + ny - 1 + 1)

    def send_z(w, src_c, h, way):
        s = shard(src_c, y, core)
        return remote(
            bufs[w].at[s, h], bufs[w].at[s, h],
            gz_send.at[w, (way + 1) // 2, src_c], gz_recv.at[w, src_c, h], at(c + way, y, core),
        )

    def send_y(w, src_c, h, e):
        s = shard(src_c, y, core)
        return remote(
            bufs[w].at[s, h], bufs[w].at[s, h],
            gy_send.at[w], gy_recv.at[w, e - 1, src_c], at(c, why(e), core),
        )

    def send_core(w, s):
        return remote(bufs[w].at[s], bufs[w].at[s], gc_send.at[w], gc_recv.at[w], core_peer)

    def spread(w, src_c, h, ways):
        for way in ways:
            @pl.when((c + way >= 0) & (c + way < nk))
            def _():
                send_z(w, src_c, h, way).start()
        loop(ny - 1, lambda e: send_y(w, src_c, h, e + 1).start())

    def forward(w, d):
        for side in (-1, 1):
            src_c = c + side * d

            @pl.when((src_c >= 0) & (src_c < nk))
            def _():
                for h in range(kb):
                    send_z(w, src_c, h, -side).wait_recv()
                    spread(w, src_c, h, (-side,))
                send_core(w, shard(src_c, y, core)).start()

    def from_y(w, first, last):
        for m in range(first, last):
            src_c = far(nk - 1 - m)

            def arrived(e):
                s = shard(src_c, why(ny - 1 - e), core)
                remote(
                    bufs[w].at[s], bufs[w].at[s], gy_send.at[w], gy_recv.at[w, e, src_c], core_peer
                ).wait_recv()
                send_core(w, s).start()

            loop(ny - 1, arrived)

    def from_core(w):
        every = bufs[w].at[pl.ds(0, nk * ny)]
        remote(every, every, gc_send.at[w], gc_recv.at[w], core_peer).wait_recv()

    def gather_sent(w):
        every = bufs[w].at[pl.ds(0, nk * ny)]
        remote(every, every, gc_send.at[w], gc_recv.at[w], core_peer).wait_send()
        if ny > 1:
            part = bufs[w].at[pl.ds(0, nk * (ny - 1))]
            remote(part, part, gy_send.at[w], gc_recv.at[w], core_peer).wait_send()
        one = bufs[w].at[0]
        for src_c in range(nk):
            @pl.when((c >= src_c) & (c + 1 < nk))
            def _():
                remote(one, one, gz_send.at[w, 1, src_c], gc_recv.at[w], core_peer).wait_send()

            @pl.when((c <= src_c) & (c >= 1))
            def _():
                remote(one, one, gz_send.at[w, 0, src_c], gc_recv.at[w], core_peer).wait_send()

    for h in range(kb):
        spread(0, c, h, (-1, 1))
    spread(1, c, 0, (-1, 1))
    send_core(0, own).start()

    for copy in staged[2 * kb :]:
        copy.wait()
    for b in range(qb):
        for h in range(H):
            q_h = q_ref[b * BLK : (b + 1) * BLK, h * HD : (h + 1) * HD]
            g_h = g_ref[b * BLK : (b + 1) * BLK, h * HD : (h + 1) * HD]
            qs[b, h * BLK : (h + 1) * BLK, :] = q_h
            gs[b, h * BLK : (h + 1) * BLK, :] = g_h
            qt[b, :, h * BLK : (h + 1) * BLK] = q_h.T
            gt[b, :, h * BLK : (h + 1) * BLK] = g_h.T

    zero_slot = qb * nnz
    kslots[zero_slot] = jnp.zeros((BLK, HD), F32)
    vslots[zero_slot] = jnp.zeros((BLK, HD), F32)
    first_row = (r * nk + c) * qb

    if nk > 1:
        forward(0, 1)
    for h in range(1, kb):
        spread(1, c, h, (-1, 1))
    send_core(1, own).start()

    def invert(j, carry):
        for b in range(qb):
            found = jnp.int32(zero_slot)
            for n in range(nnz):
                found = jnp.where(pat_ref[n, first_row + b] == j, b * nnz + n, found)
            inv[b, j] = found
        return carry

    for d in range(2, nk):
        forward(0, d)
        forward(1, d - 1)
        if d == 2:
            lax.fori_loop(0, key_blocks, invert, 0)
    if nk < 3:
        lax.fori_loop(0, key_blocks, invert, 0)
    from_y(0, 0, nk - 1)
    if nk > 1:
        forward(1, nk - 1)
    from_y(0, nk - 1, nk)
    from_core(0)

    def partial(w, s, half):
        j = s * kb + half
        value = slots[w][inv[0, j]]
        for b in range(1, qb):
            value = value + slots[w][inv[b, j]]
        return value

    def to_core(w, i, s):
        return remote(outs[w].at[s], core_in.at[w, i], core_send.at[w], core_recv.at[w, i], core_peer)

    def to_y(w, i, s, half, where):
        return remote(
            outs[w].at[s, half], y_in.at[w, i, half], y_send.at[w], y_recv.at[w, i, half], where
        )

    def to_z(w, s, half, where):
        return remote(outs[w].at[s, half], z_in.at[w, c, half], z_send.at[w], z_recv.at[w], where)

    def place(i):
        return far(i % nk), why((i // nk + 1) % ny)

    y_sends = nk * (ny - 1)

    def core_step(w):
        def step(i):
            c_at, y_at = place(i)
            s = shard(c_at, y_at, other)
            for half in range(kb):
                outs[w][s, half] = partial(w, s, half).astype(BF16)
            to_core(w, i, s).start()

        loop(nk * ny, step)

    def y_step(w):
        def step(i):
            c_at, y_at = place(i)
            s = shard(c_at, y_at, core)
            to_core(w, i, s).wait_recv()
            for half in range(kb):
                value = partial(w, s, half) + core_in[w, i, half].astype(F32)
                outs[w][s, half] = value.astype(BF16)
                to_y(w, i, s, half, at(c, y_at, core)).start()

        loop(y_sends, step)

    def summed(w, k, s, half):
        value = partial(w, s, half) + core_in[w, y_sends + k, half].astype(F32)
        for e in range(1, ny):
            value = value + y_in[w, (e - 1) * nk + k, half].astype(F32)
        return value

    def landed(w, k, s, half):
        if half == 0:
            to_core(w, y_sends + k, s).wait_recv()
        for e in range(1, ny):
            to_y(w, (e - 1) * nk + k, s, half, core_peer).wait_recv()

    def z_step(w, k):
        c_at = far(k)
        s = shard(c_at, y, core)
        for half in range(kb):
            landed(w, k, s, half)
            outs[w][s, half] = summed(w, k, s, half).astype(BF16)
            to_z(w, s, half, at(c_at, y, core)).start()

    def finish(w, out):
        for half in range(kb):
            landed(w, nk - 1, own, half)
        if nk > 1:
            some = z_in.at[w, pl.ds(0, nk - 1)]
            remote(some, some, z_send.at[w], z_recv.at[w], core_peer).wait_recv()
        for half in range(kb):
            value = summed(w, nk - 1, own, half)
            for d in range(1, nk):
                value = value + z_in[w, zed(d), half].astype(F32)
            out[half * BLK : (half + 1) * BLK, :] = value.astype(BF16)

    def reduction_sent(w):
        every = outs[w].at[pl.ds(0, nk * ny)]
        remote(every, every, core_send.at[w], z_recv.at[w], core_peer).wait_send()
        if ny > 1:
            part = outs[w].at[pl.ds(0, y_sends)]
            remote(part, part, y_send.at[w], z_recv.at[w], core_peer).wait_send()
        if nk > 1:
            part = outs[w].at[pl.ds(0, nk - 1)]
            remote(part, part, z_send.at[w], z_recv.at[w], core_peer).wait_send()

    def query_results(b):
        attended = att_scr[b]
        grad_q = jnp.zeros((HD, H * BLK), F32)
        for n in range(0, nnz, chunk):
            part = slice(n * BLK, n * BLK + rows)
            grad_q = grad_q + dot_t(kc_scr[b, part, :], ds_scr[b, part, :])
        grad_q = (grad_q * scaling).astype(BF16)
        for h in range(H):
            o_ref[b * BLK : (b + 1) * BLK, h * HD : (h + 1) * HD] = attended[
                :, h * BLK : (h + 1) * BLK
            ].T
            dq_ref[b * BLK : (b + 1) * BLK, h * HD : (h + 1) * HD] = grad_q[
                :, h * BLK : (h + 1) * BLK
            ].T

    for b in range(qb):
        for n in range(nnz):
            j = pat_ref[n, first_row + b]
            kc_scr[b, n * BLK : (n + 1) * BLK, :] = kbuf[j // kb, j % kb]
        top = None
        for n in range(0, nnz, chunk):
            part = slice(n * BLK, n * BLK + rows)
            scores = dot(kc_scr[b, part, :], qt[b])
            s_scr[b, part, :] = scores
            high = jnp.max(scores, axis=0, keepdims=True)
            top = high if top is None else jnp.maximum(top, high)
        total = jnp.zeros((1, H * BLK), F32)
        for n in range(0, nnz, chunk):
            part = slice(n * BLK, n * BLK + rows)
            weights = jnp.exp2((s_scr[b, part, :] - top) * (scaling * math.log2(math.e)))
            s_scr[b, part, :] = weights
            total = total + jnp.sum(weights, axis=0, keepdims=True)
        share = 1.0 / total
        share_scr[b, 0:1, :] = share
        share_scr[b, 1:2, :] = total
        for n in range(0, nnz, chunk):
            part = slice(n * BLK, n * BLK + rows)
            grad_v = dot((s_scr[b, part, :] * share).astype(BF16), gs[b])
            for i in range(chunk):
                vslots[b * nnz + n + i] = grad_v[i * BLK : (i + 1) * BLK]

    if tight:
        gather_sent(0)
    core_step(1)
    from_y(1, 0, nk)
    y_step(1)
    if not tight:
        gather_sent(0)
    from_core(1)

    for b in range(qb):
        for n in range(nnz):
            j = pat_ref[n, first_row + b]
            vc_scr[b, n * BLK : (n + 1) * BLK, :] = vbuf[j // kb, j % kb]
        mix = jnp.zeros((HD, H * BLK), F32)
        for n in range(0, nnz, chunk):
            part = slice(n * BLK, n * BLK + rows)
            mix = mix + dot_t(vc_scr[b, part, :], s_scr[b, part, :].astype(BF16))
        share = share_scr[b, 0:1, :]
        attended = (mix / share_scr[b, 1:2, :]).astype(BF16)
        delta = jnp.sum(gt[b].astype(F32) * attended.astype(F32), axis=0, keepdims=True)
        att_scr[b] = attended
        for n in range(0, nnz, chunk):
            part = slice(n * BLK, n * BLK + rows)
            grad_prob = dot(vc_scr[b, part, :], gt[b])
            prob = s_scr[b, part, :] * share
            grad_score = (prob * (grad_prob - delta)).astype(BF16)
            grad_k = dot(grad_score, qs[b]) * scaling
            ds_scr[b, part, :] = grad_score
            for i in range(chunk):
                kslots[b * nnz + n + i] = grad_k[i * BLK : (i + 1) * BLK]

    if tight:
        gather_sent(1)
    core_step(0)
    if nk > 1:
        z_step(1, 0)
    y_step(0)
    for k in range(1, nk - 1):
        z_step(1, k)
    if not tight:
        gather_sent(1)
    if nk > 1:
        z_step(0, 0)
    finish(1, dv_ref)
    for k in range(1, nk - 1):
        z_step(0, k)
    for b in range(qb):
        query_results(b)
    reduction_sent(1)
    finish(0, dk_ref)
    reduction_sent(0)


def write_out(*refs):
    half = len(refs) // 2
    sem = refs[-1]
    copies = [
        pltpu.make_async_copy(src, dst, sem.at[i])
        for i, (src, dst) in enumerate(zip(refs[:half], refs[half:-1]))
    ]
    for copy in copies:
        copy.start()
    for copy in copies:
        copy.wait()


def to_hbm(results):
    n = len(results)
    return pl.pallas_call(
        write_out,
        out_shape=tuple(jax.ShapeDtypeStruct(a.shape, a.dtype) for a in results),
        in_specs=[pl.BlockSpec(memory_space=pltpu.VMEM)] * n,
        out_specs=(pl.BlockSpec(memory_space=pl.ANY),) * n,
        scratch_shapes=[pltpu.SemaphoreType.DMA((n,))],
        compiler_params=pltpu.CompilerParams(vmem_limit_bytes=4 * 1024 * 1024),
    )(*results)


def body(nq, nk, queries, keys, values, out_grad, pattern):
    pattern = pattern.T
    nnz = pattern.shape[0]
    ny = nq // 2
    qb = queries.shape[0] // BLK
    kb = keys.shape[0] // BLK
    shards = nq * nk
    block = (kb, BLK, HD)
    y_sends = max(nk * (ny - 1), 1)
    dma = pltpu.SemaphoreType.DMA
    vmem = pl.BlockSpec(memory_space=pltpu.VMEM)
    results = pl.pallas_call(
        functools.partial(kernel, nq, nk, nnz),
        out_shape=(
            pltpu.VMEM(queries.shape, BF16),
            pltpu.VMEM(queries.shape, BF16),
            pltpu.VMEM(keys.shape, BF16),
            pltpu.VMEM(keys.shape, BF16),
        ),
        in_specs=[pl.BlockSpec(memory_space=pl.ANY)] * 4 + [pl.BlockSpec(memory_space=pltpu.SMEM)],
        out_specs=(vmem,) * 4,
        scratch_shapes=[
            pltpu.VMEM(queries.shape, BF16),
            pltpu.VMEM(queries.shape, BF16),
            pltpu.VMEM((shards,) + block, BF16),
            pltpu.VMEM((shards,) + block, BF16),
            pltpu.VMEM((shards if shards <= 64 else 1,) + block, BF16),
            pltpu.VMEM((2, nk * ny) + block, BF16),
            pltpu.VMEM((2, y_sends) + block, BF16),
            pltpu.VMEM((2, nk) + block, BF16),
            pltpu.VMEM((qb * nnz + 1, BLK, HD), F32),
            pltpu.VMEM((qb * nnz + 1, BLK, HD), F32),
            pltpu.VMEM((qb, nnz * BLK, H * BLK), F32),
            pltpu.VMEM((qb, 8, H * BLK), F32),
            pltpu.VMEM((qb, H * BLK, HD), BF16),
            pltpu.VMEM((qb, H * BLK, HD), BF16),
            pltpu.VMEM((qb, HD, H * BLK), BF16),
            pltpu.VMEM((qb, HD, H * BLK), BF16),
            pltpu.VMEM((qb, nnz * BLK, HD), BF16),
            pltpu.VMEM((qb, nnz * BLK, HD), BF16),
            pltpu.VMEM((qb, HD, H * BLK), BF16),
            pltpu.VMEM((qb, nnz * BLK, H * BLK), BF16),
            pltpu.SMEM((qb, shards * kb), jnp.int32),
            dma((2 * kb + 2,)),
            dma((2, 2, nk)),
            dma((2, nk, kb)),
            dma((2,)),
            dma((2, max(ny - 1, 1), nk)),
            dma((2,)),
            dma((2,)),
            dma((2,)),
            dma((2, nk * ny)),
            dma((2,)),
            dma((2, y_sends, kb)),
            dma((2,)),
            dma((2,)),
        ],
        compiler_params=pltpu.CompilerParams(
            collective_id=0, has_side_effects=True, vmem_limit_bytes=60 * 1024 * 1024
        ),
    )(queries, out_grad, keys, values, pattern)
    return to_hbm(results)


def solution(mesh):
    return jax.shard_map(
        functools.partial(body, mesh.shape["qrow"], mesh.shape["kcol"]),
        mesh=mesh,
        in_specs=(
            P(("groups", "qrow", "kcol"), None),
            P(("groups", "kcol", "qrow"), None),
            P(("groups", "kcol", "qrow"), None),
            P(("groups", "qrow", "kcol"), None),
            P("groups", None),
        ),
        out_specs=(
            P(("groups", "qrow", "kcol"), None),
            P(("groups", "qrow", "kcol"), None),
            P(("groups", "kcol", "qrow"), None),
            P(("groups", "kcol", "qrow"), None),
        ),
        check_vma=False,
    )
```

```python
import functools
import math

import jax
import jax.numpy as jnp
from jax import lax
from jax.experimental import pallas as pl
from jax.experimental.pallas import tpu as pltpu
from jax.sharding import PartitionSpec as P

H = 4
HD = 128
BLK = 128
MESH = pl.DeviceIdType.MESH
F32 = jnp.float32
BF16 = jnp.bfloat16


def dot(a, b):
    return jnp.dot(a, b, preferred_element_type=F32)


def dot_t(a, b):
    return lax.dot_general(a, b, (((0,), (0,)), ((), ())), preferred_element_type=F32)


def kernel(
    nq, nk, nnz, q_hbm, g_hbm, k_hbm, v_hbm, pat_hbm, o_ref, dq_ref, dk_ref, dv_ref,
    q_ref, g_ref, kbuf, vbuf, vout, core_in, y_in, z_in, kslots, vslots, s_scr, share_scr,
    qs, gs, qt, gt, kc_scr, vc_scr, att_scr, ds_scr, pat_ref, inv,
    in_sem, gz_send, gz_recv, gy_send, gy_recv, gc_send, gc_recv,
    core_send, core_recv, y_send, y_recv, z_send, z_recv,
):
    ny = nq // 2
    qb = q_ref.shape[0] // BLK
    kb = kbuf.shape[1]
    key_blocks = nq * nk * kb
    chunk = 2 if nnz % 2 == 0 else 1
    rows = chunk * BLK
    scaling = HD ** (-0.5)
    bufs = (kbuf, vbuf)
    tight = vout.shape[0] < kbuf.shape[0]
    outs = (vbuf, kbuf) if tight else (kbuf, vout)
    slots = (kslots, vslots)
    r = lax.axis_index("qrow")
    c = lax.axis_index("kcol")
    y, core = r // 2, r % 2
    other = 1 - core

    def loop(n, step):
        if n <= 8:
            for i in range(n):
                step(i)
        else:
            lax.fori_loop(0, n, lambda i, carry: (step(i), carry)[1], 0)

    def shard(c_at, y_at, core_at):
        return c_at * nq + y_at * 2 + core_at

    def zed(d):
        return (c + d) % nk

    def why(e):
        return (y + e) % ny

    def at(c_to, y_to, core_to):
        return {"qrow": y_to * 2 + core_to, "kcol": c_to}

    low_half = 1 - (2 * c) // nk

    def far(k):
        up, down = k, nk - 1 - k
        up = up + (nk + up - c) // nk
        down = down - (nk + c - down) // nk
        picked = low_half * down + (1 - low_half) * up
        last = k // (nk - 1) if nk > 1 else 1
        return last * c + (1 - last) * picked

    def remote(src, dst, send, recv, where):
        return pltpu.make_async_remote_copy(
            src_ref=src, dst_ref=dst, send_sem=send, recv_sem=recv,
            device_id=where, device_id_type=MESH,
        )

    core_peer = at(c, y, other)
    own = shard(c, y, core)

    barrier = pltpu.get_barrier_semaphore()
    for d in range(1, nk):
        pl.semaphore_signal(barrier, inc=1, device_id=at(zed(d), y, core), device_id_type=MESH)
    for e in range(1, ny):
        pl.semaphore_signal(barrier, inc=1, device_id=at(c, why(e), core), device_id_type=MESH)
    pl.semaphore_signal(barrier, inc=1, device_id=core_peer, device_id_type=MESH)

    staged = []
    for w, src in ((0, k_hbm), (1, v_hbm)):
        for h in range(kb):
            staged.append(
                pltpu.make_async_copy(
                    src.at[pl.ds(h * BLK, BLK)], bufs[w].at[own, h], in_sem.at[w * kb + h]
                )
            )
    staged.append(pltpu.make_async_copy(q_hbm, q_ref, in_sem.at[2 * kb]))
    staged.append(pltpu.make_async_copy(g_hbm, g_ref, in_sem.at[2 * kb + 1]))
    staged.append(pltpu.make_async_copy(pat_hbm, pat_ref, in_sem.at[2 * kb + 2]))
    for copy in staged:
        copy.start()
    for copy in staged[: 2 * kb]:
        copy.wait()
    pl.semaphore_wait(barrier, nk - 1 + ny - 1 + 1)

    def send_z(w, src_c, h, way):
        s = shard(src_c, y, core)
        return remote(
            bufs[w].at[s, h], bufs[w].at[s, h],
            gz_send.at[w, (way + 1) // 2, src_c], gz_recv.at[w, src_c, h], at(c + way, y, core),
        )

    def send_y(w, src_c, h, e):
        s = shard(src_c, y, core)
        return remote(
            bufs[w].at[s, h], bufs[w].at[s, h],
            gy_send.at[w], gy_recv.at[w, e - 1, src_c], at(c, why(e), core),
        )

    def send_core(w, s):
        return remote(bufs[w].at[s], bufs[w].at[s], gc_send.at[w], gc_recv.at[w], core_peer)

    def spread(w, src_c, h, ways):
        for way in ways:
            @pl.when((c + way >= 0) & (c + way < nk))
            def _():
                send_z(w, src_c, h, way).start()
        loop(ny - 1, lambda e: send_y(w, src_c, h, e + 1).start())

    def forward(w, d):
        for side in (-1, 1):
            src_c = c + side * d

            @pl.when((src_c >= 0) & (src_c < nk))
            def _():
                for h in range(kb):
                    send_z(w, src_c, h, -side).wait_recv()
                    spread(w, src_c, h, (-side,))
                send_core(w, shard(src_c, y, core)).start()

    def from_y(w, first, last):
        for m in range(first, last):
            src_c = far(nk - 1 - m)

            def arrived(e):
                s = shard(src_c, why(ny - 1 - e), core)
                remote(
                    bufs[w].at[s], bufs[w].at[s], gy_send.at[w], gy_recv.at[w, e, src_c], core_peer
                ).wait_recv()
                send_core(w, s).start()

            loop(ny - 1, arrived)

    def from_core(w):
        every = bufs[w].at[pl.ds(0, nk * ny)]
        remote(every, every, gc_send.at[w], gc_recv.at[w], core_peer).wait_recv()

    def gather_sent(w):
        every = bufs[w].at[pl.ds(0, nk * ny)]
        remote(every, every, gc_send.at[w], gc_recv.at[w], core_peer).wait_send()
        if ny > 1:
            part = bufs[w].at[pl.ds(0, nk * (ny - 1))]
            remote(part, part, gy_send.at[w], gc_recv.at[w], core_peer).wait_send()
        one = bufs[w].at[0]
        for src_c in range(nk):
            @pl.when((c >= src_c) & (c + 1 < nk))
            def _():
                remote(one, one, gz_send.at[w, 1, src_c], gc_recv.at[w], core_peer).wait_send()

            @pl.when((c <= src_c) & (c >= 1))
            def _():
                remote(one, one, gz_send.at[w, 0, src_c], gc_recv.at[w], core_peer).wait_send()

    for h in range(kb):
        spread(0, c, h, (-1, 1))
    spread(1, c, 0, (-1, 1))
    send_core(0, own).start()

    for copy in staged[2 * kb :]:
        copy.wait()
    for b in range(qb):
        for h in range(H):
            q_h = q_ref[b * BLK : (b + 1) * BLK, h * HD : (h + 1) * HD]
            g_h = g_ref[b * BLK : (b + 1) * BLK, h * HD : (h + 1) * HD]
            qs[b, h * BLK : (h + 1) * BLK, :] = q_h
            gs[b, h * BLK : (h + 1) * BLK, :] = g_h
            qt[b, :, h * BLK : (h + 1) * BLK] = q_h.T
            gt[b, :, h * BLK : (h + 1) * BLK] = g_h.T

    zero_slot = qb * nnz
    kslots[zero_slot] = jnp.zeros((BLK, HD), F32)
    vslots[zero_slot] = jnp.zeros((BLK, HD), F32)
    first_row = (r * nk + c) * qb

    if nk > 1:
        forward(0, 1)
    for h in range(1, kb):
        spread(1, c, h, (-1, 1))
    send_core(1, own).start()

    def invert(j, carry):
        for b in range(qb):
            found = jnp.int32(zero_slot)
            for n in range(nnz):
                found = jnp.where(pat_ref[n, first_row + b] == j, b * nnz + n, found)
            inv[b, j] = found
        return carry

    for d in range(2, nk):
        forward(0, d)
        forward(1, d - 1)
        if d == 2:
            lax.fori_loop(0, key_blocks, invert, 0)
    if nk < 3:
        lax.fori_loop(0, key_blocks, invert, 0)
    from_y(0, 0, nk - 1)
    if nk > 1:
        forward(1, nk - 1)
    from_y(0, nk - 1, nk)
    from_core(0)

    def partial(w, s, half):
        j = s * kb + half
        value = slots[w][inv[0, j]]
        for b in range(1, qb):
            value = value + slots[w][inv[b, j]]
        return value

    def to_core(w, i, s):
        return remote(outs[w].at[s], core_in.at[w, i], core_send.at[w], core_recv.at[w, i], core_peer)

    def to_y(w, i, s, half, where):
        return remote(
            outs[w].at[s, half], y_in.at[w, i, half], y_send.at[w], y_recv.at[w, i, half], where
        )

    def to_z(w, s, half, where):
        return remote(outs[w].at[s, half], z_in.at[w, c, half], z_send.at[w], z_recv.at[w], where)

    def place(i):
        return far(i % nk), why((i // nk + 1) % ny)

    y_sends = nk * (ny - 1)

    def core_step(w):
        def step(i):
            c_at, y_at = place(i)
            s = shard(c_at, y_at, other)
            for half in range(kb):
                outs[w][s, half] = partial(w, s, half).astype(BF16)
            to_core(w, i, s).start()

        loop(nk * ny, step)

    def y_step(w):
        def step(i):
            c_at, y_at = place(i)
            s = shard(c_at, y_at, core)
            to_core(w, i, s).wait_recv()
            for half in range(kb):
                value = partial(w, s, half) + core_in[w, i, half].astype(F32)
                outs[w][s, half] = value.astype(BF16)
                to_y(w, i, s, half, at(c, y_at, core)).start()

        loop(y_sends, step)

    def summed(w, k, s, half):
        value = partial(w, s, half) + core_in[w, y_sends + k, half].astype(F32)
        for e in range(1, ny):
            value = value + y_in[w, (e - 1) * nk + k, half].astype(F32)
        return value

    def landed(w, k, s, half):
        if half == 0:
            to_core(w, y_sends + k, s).wait_recv()
        for e in range(1, ny):
            to_y(w, (e - 1) * nk + k, s, half, core_peer).wait_recv()

    def z_step(w, k):
        c_at = far(k)
        s = shard(c_at, y, core)
        for half in range(kb):
            landed(w, k, s, half)
            outs[w][s, half] = summed(w, k, s, half).astype(BF16)
            to_z(w, s, half, at(c_at, y, core)).start()

    def finish(w, out):
        for half in range(kb):
            landed(w, nk - 1, own, half)
        if nk > 1:
            some = z_in.at[w, pl.ds(0, nk - 1)]
            remote(some, some, z_send.at[w], z_recv.at[w], core_peer).wait_recv()
        for half in range(kb):
            value = summed(w, nk - 1, own, half)
            for d in range(1, nk):
                value = value + z_in[w, zed(d), half].astype(F32)
            out[half * BLK : (half + 1) * BLK, :] = value.astype(BF16)

    def reduction_sent(w):
        every = outs[w].at[pl.ds(0, nk * ny)]
        remote(every, every, core_send.at[w], z_recv.at[w], core_peer).wait_send()
        if ny > 1:
            part = outs[w].at[pl.ds(0, y_sends)]
            remote(part, part, y_send.at[w], z_recv.at[w], core_peer).wait_send()
        if nk > 1:
            part = outs[w].at[pl.ds(0, nk - 1)]
            remote(part, part, z_send.at[w], z_recv.at[w], core_peer).wait_send()

    def query_results(b):
        attended = att_scr[b]
        grad_q = jnp.zeros((HD, H * BLK), F32)
        for n in range(0, nnz, chunk):
            part = slice(n * BLK, n * BLK + rows)
            grad_q = grad_q + dot_t(kc_scr[b, part, :], ds_scr[b, part, :])
        grad_q = (grad_q * scaling).astype(BF16)
        for h in range(H):
            o_ref[b * BLK : (b + 1) * BLK, h * HD : (h + 1) * HD] = attended[
                :, h * BLK : (h + 1) * BLK
            ].T
            dq_ref[b * BLK : (b + 1) * BLK, h * HD : (h + 1) * HD] = grad_q[
                :, h * BLK : (h + 1) * BLK
            ].T

    for b in range(qb):
        for n in range(nnz):
            j = pat_ref[n, first_row + b]
            kc_scr[b, n * BLK : (n + 1) * BLK, :] = kbuf[j // kb, j % kb]
        top = None
        for n in range(0, nnz, chunk):
            part = slice(n * BLK, n * BLK + rows)
            scores = dot(kc_scr[b, part, :], qt[b])
            s_scr[b, part, :] = scores
            high = jnp.max(scores, axis=0, keepdims=True)
            top = high if top is None else jnp.maximum(top, high)
        total = jnp.zeros((1, H * BLK), F32)
        for n in range(0, nnz, chunk):
            part = slice(n * BLK, n * BLK + rows)
            weights = jnp.exp2((s_scr[b, part, :] - top) * (scaling * math.log2(math.e)))
            s_scr[b, part, :] = weights
            total = total + jnp.sum(weights, axis=0, keepdims=True)
        share = 1.0 / total
        share_scr[b, 0:1, :] = share
        share_scr[b, 1:2, :] = total
        for n in range(0, nnz, chunk):
            part = slice(n * BLK, n * BLK + rows)
            grad_v = dot((s_scr[b, part, :] * share).astype(BF16), gs[b])
            for i in range(chunk):
                vslots[b * nnz + n + i] = grad_v[i * BLK : (i + 1) * BLK]

    if tight:
        gather_sent(0)
    core_step(1)
    from_y(1, 0, nk)
    y_step(1)
    if not tight:
        gather_sent(0)
    from_core(1)

    for b in range(qb):
        for n in range(nnz):
            j = pat_ref[n, first_row + b]
            vc_scr[b, n * BLK : (n + 1) * BLK, :] = vbuf[j // kb, j % kb]
        mix = jnp.zeros((HD, H * BLK), F32)
        for n in range(0, nnz, chunk):
            part = slice(n * BLK, n * BLK + rows)
            mix = mix + dot_t(vc_scr[b, part, :], s_scr[b, part, :].astype(BF16))
        share = share_scr[b, 0:1, :]
        attended = (mix / share_scr[b, 1:2, :]).astype(BF16)
        delta = jnp.sum(gt[b].astype(F32) * attended.astype(F32), axis=0, keepdims=True)
        att_scr[b] = attended
        for n in range(0, nnz, chunk):
            part = slice(n * BLK, n * BLK + rows)
            grad_prob = dot(vc_scr[b, part, :], gt[b])
            prob = s_scr[b, part, :] * share
            grad_score = (prob * (grad_prob - delta)).astype(BF16)
            grad_k = dot(grad_score, qs[b]) * scaling
            ds_scr[b, part, :] = grad_score
            for i in range(chunk):
                kslots[b * nnz + n + i] = grad_k[i * BLK : (i + 1) * BLK]

    if tight:
        gather_sent(1)
    core_step(0)
    if nk > 1:
        z_step(1, 0)
    y_step(0)
    for k in range(1, nk - 1):
        z_step(1, k)
    if not tight:
        gather_sent(1)
    if nk > 1:
        z_step(0, 0)
    finish(1, dv_ref)
    for k in range(1, nk - 1):
        z_step(0, k)
    for b in range(qb):
        query_results(b)
    reduction_sent(1)
    finish(0, dk_ref)
    reduction_sent(0)


def write_out(*refs):
    half = len(refs) // 2
    sem = refs[-1]
    copies = [
        pltpu.make_async_copy(src, dst, sem.at[i])
        for i, (src, dst) in enumerate(zip(refs[:half], refs[half:-1]))
    ]
    for copy in copies:
        copy.start()
    for copy in copies:
        copy.wait()


def to_hbm(results):
    n = len(results)
    return pl.pallas_call(
        write_out,
        out_shape=tuple(jax.ShapeDtypeStruct(a.shape, a.dtype) for a in results),
        in_specs=[pl.BlockSpec(memory_space=pltpu.VMEM)] * n,
        out_specs=(pl.BlockSpec(memory_space=pl.ANY),) * n,
        scratch_shapes=[pltpu.SemaphoreType.DMA((n,))],
        compiler_params=pltpu.CompilerParams(vmem_limit_bytes=4 * 1024 * 1024),
    )(*results)


def body(nq, nk, queries, keys, values, out_grad, pattern):
    pattern = pattern.T
    nnz = pattern.shape[0]
    ny = nq // 2
    qb = queries.shape[0] // BLK
    kb = keys.shape[0] // BLK
    shards = nq * nk
    block = (kb, BLK, HD)
    y_sends = max(nk * (ny - 1), 1)
    dma = pltpu.SemaphoreType.DMA
    vmem = pl.BlockSpec(memory_space=pltpu.VMEM)
    results = pl.pallas_call(
        functools.partial(kernel, nq, nk, nnz),
        out_shape=(
            pltpu.VMEM(queries.shape, BF16),
            pltpu.VMEM(queries.shape, BF16),
            pltpu.VMEM(keys.shape, BF16),
            pltpu.VMEM(keys.shape, BF16),
        ),
        in_specs=[pl.BlockSpec(memory_space=pl.ANY)] * 5,
        out_specs=(vmem,) * 4,
        scratch_shapes=[
            pltpu.VMEM(queries.shape, BF16),
            pltpu.VMEM(queries.shape, BF16),
            pltpu.VMEM((shards,) + block, BF16),
            pltpu.VMEM((shards,) + block, BF16),
            pltpu.VMEM((shards if shards <= 64 else 1,) + block, BF16),
            pltpu.VMEM((2, nk * ny) + block, BF16),
            pltpu.VMEM((2, y_sends) + block, BF16),
            pltpu.VMEM((2, nk) + block, BF16),
            pltpu.VMEM((qb * nnz + 1, BLK, HD), F32),
            pltpu.VMEM((qb * nnz + 1, BLK, HD), F32),
            pltpu.VMEM((qb, nnz * BLK, H * BLK), F32),
            pltpu.VMEM((qb, 8, H * BLK), F32),
            pltpu.VMEM((qb, H * BLK, HD), BF16),
            pltpu.VMEM((qb, H * BLK, HD), BF16),
            pltpu.VMEM((qb, HD, H * BLK), BF16),
            pltpu.VMEM((qb, HD, H * BLK), BF16),
            pltpu.VMEM((qb, nnz * BLK, HD), BF16),
            pltpu.VMEM((qb, nnz * BLK, HD), BF16),
            pltpu.VMEM((qb, HD, H * BLK), BF16),
            pltpu.VMEM((qb, nnz * BLK, H * BLK), BF16),
            pltpu.SMEM(pattern.shape, jnp.int32),
            pltpu.SMEM((qb, shards * kb), jnp.int32),
            dma((2 * kb + 3,)),
            dma((2, 2, nk)),
            dma((2, nk, kb)),
            dma((2,)),
            dma((2, max(ny - 1, 1), nk)),
            dma((2,)),
            dma((2,)),
            dma((2,)),
            dma((2, nk * ny)),
            dma((2,)),
            dma((2, y_sends, kb)),
            dma((2,)),
            dma((2,)),
        ],
        compiler_params=pltpu.CompilerParams(
            collective_id=0, has_side_effects=True, vmem_limit_bytes=60 * 1024 * 1024
        ),
    )(queries, out_grad, keys, values, pattern)
    return to_hbm(results)


def solution(mesh):
    return jax.shard_map(
        functools.partial(body, mesh.shape["qrow"], mesh.shape["kcol"]),
        mesh=mesh,
        in_specs=(
            P(("groups", "qrow", "kcol"), None),
            P(("groups", "kcol", "qrow"), None),
            P(("groups", "kcol", "qrow"), None),
            P(("groups", "qrow", "kcol"), None),
            P("groups", None),
        ),
        out_specs=(
            P(("groups", "qrow", "kcol"), None),
            P(("groups", "qrow", "kcol"), None),
            P(("groups", "kcol", "qrow"), None),
            P(("groups", "kcol", "qrow"), None),
        ),
        check_vma=False,
    )
```

```python
import functools
import math

import jax
import jax.numpy as jnp
from jax import lax
from jax.experimental import pallas as pl
from jax.experimental.pallas import tpu as pltpu
from jax.sharding import PartitionSpec as P

H = 4
HD = 128
BLK = 128
MESH = pl.DeviceIdType.MESH
F32 = jnp.float32
BF16 = jnp.bfloat16


def dot(a, b):
    return jnp.dot(a, b, preferred_element_type=F32)


def dot_t(a, b):
    return lax.dot_general(a, b, (((0,), (0,)), ((), ())), preferred_element_type=F32)


def kernel(
    nq, nk, nnz, q_hbm, g_hbm, k_hbm, v_hbm, pat_hbm, o_ref, dq_ref, dk_ref, dv_ref,
    q_ref, g_ref, kbuf, vbuf, vout, core_in, y_in, z_in, kslots, vslots, s_scr, share_scr,
    qs, gs, qt, gt, kc_scr, vc_scr, att_scr, ds_scr, pat_ref, inv,
    in_sem, gz_send, gz_recv, gy_send, gy_recv, gc_send, gc_recv,
    core_send, core_recv, y_send, y_recv, z_send, z_recv,
):
    ny = nq // 2
    qb = q_ref.shape[0] // BLK
    kb = kbuf.shape[1]
    key_blocks = nq * nk * kb
    chunk = 2 if nnz % 2 == 0 else 1
    rows = chunk * BLK
    scaling = HD ** (-0.5)
    bufs = (kbuf, vbuf)
    tight = vout.shape[0] < kbuf.shape[0]
    outs = (vbuf, kbuf) if tight else (kbuf, vout)
    slots = (kslots, vslots)
    r = lax.axis_index("qrow")
    c = lax.axis_index("kcol")
    y, core = r // 2, r % 2
    other = 1 - core

    def loop(n, step):
        if n <= 8:
            for i in range(n):
                step(i)
        else:
            lax.fori_loop(0, n, lambda i, carry: (step(i), carry)[1], 0)

    def shard(c_at, y_at, core_at):
        return c_at * nq + y_at * 2 + core_at

    def zed(d):
        return (c + d) % nk

    def why(e):
        return (y + e) % ny

    def at(c_to, y_to, core_to):
        return {"qrow": y_to * 2 + core_to, "kcol": c_to}

    low_half = 1 - (2 * c) // nk

    def far(k):
        up, down = k, nk - 1 - k
        up = up + (nk + up - c) // nk
        down = down - (nk + c - down) // nk
        picked = low_half * down + (1 - low_half) * up
        last = k // (nk - 1) if nk > 1 else 1
        return last * c + (1 - last) * picked

    def remote(src, dst, send, recv, where):
        return pltpu.make_async_remote_copy(
            src_ref=src, dst_ref=dst, send_sem=send, recv_sem=recv,
            device_id=where, device_id_type=MESH,
        )

    core_peer = at(c, y, other)
    own = shard(c, y, core)

    barrier = pltpu.get_barrier_semaphore()
    for d in range(1, nk):
        pl.semaphore_signal(barrier, inc=1, device_id=at(zed(d), y, core), device_id_type=MESH)
    for e in range(1, ny):
        pl.semaphore_signal(barrier, inc=1, device_id=at(c, why(e), core), device_id_type=MESH)
    pl.semaphore_signal(barrier, inc=1, device_id=core_peer, device_id_type=MESH)

    staged = []
    for w, src in ((0, k_hbm), (1, v_hbm)):
        for h in range(kb):
            staged.append(
                pltpu.make_async_copy(
                    src.at[pl.ds(h * BLK, BLK)], bufs[w].at[own, h], in_sem.at[w * kb + h]
                )
            )
    staged.append(pltpu.make_async_copy(q_hbm, q_ref, in_sem.at[2 * kb]))
    staged.append(pltpu.make_async_copy(g_hbm, g_ref, in_sem.at[2 * kb + 1]))
    staged.append(pltpu.make_async_copy(pat_hbm, pat_ref, in_sem.at[2 * kb + 2]))
    for copy in staged:
        copy.start()
    for copy in staged[:kb]:
        copy.wait()
    pl.semaphore_wait(barrier, nk - 1 + ny - 1 + 1)

    pieces = 2 * kb

    def piece(w, s, h):
        return bufs[w].at[s, h // 2, pl.ds(h % 2 * (BLK // 2), BLK // 2)]

    def send_z(w, src_c, h, way):
        s = shard(src_c, y, core)
        return remote(
            piece(w, s, h), piece(w, s, h),
            gz_send.at[w, (way + 1) // 2, src_c], gz_recv.at[w, src_c, h], at(c + way, y, core),
        )

    def send_y(w, src_c, h, e):
        s = shard(src_c, y, core)
        return remote(
            piece(w, s, h), piece(w, s, h),
            gy_send.at[w], gy_recv.at[w, e - 1, src_c], at(c, why(e), core),
        )

    def send_core(w, s):
        return remote(bufs[w].at[s], bufs[w].at[s], gc_send.at[w], gc_recv.at[w], core_peer)

    def spread(w, src_c, h, ways):
        for way in ways:
            @pl.when((c + way >= 0) & (c + way < nk))
            def _():
                send_z(w, src_c, h, way).start()
        loop(ny - 1, lambda e: send_y(w, src_c, h, e + 1).start())

    def forward(w, d):
        for side in (-1, 1):
            src_c = c + side * d

            @pl.when((src_c >= 0) & (src_c < nk))
            def _():
                for h in range(pieces):
                    send_z(w, src_c, h, -side).wait_recv()
                    spread(w, src_c, h, (-side,))
                send_core(w, shard(src_c, y, core)).start()

    def from_y(w, first, last):
        for m in range(first, last):
            src_c = far(nk - 1 - m)

            def arrived(e):
                s = shard(src_c, why(ny - 1 - e), core)
                remote(
                    bufs[w].at[s], bufs[w].at[s], gy_send.at[w], gy_recv.at[w, e, src_c], core_peer
                ).wait_recv()
                send_core(w, s).start()

            loop(ny - 1, arrived)

    def from_core(w):
        every = bufs[w].at[pl.ds(0, nk * ny)]
        remote(every, every, gc_send.at[w], gc_recv.at[w], core_peer).wait_recv()

    def gather_sent(w):
        every = bufs[w].at[pl.ds(0, nk * ny)]
        remote(every, every, gc_send.at[w], gc_recv.at[w], core_peer).wait_send()
        if ny > 1:
            part = bufs[w].at[pl.ds(0, nk * (ny - 1))]
            remote(part, part, gy_send.at[w], gc_recv.at[w], core_peer).wait_send()
        one = bufs[w].at[0]
        for src_c in range(nk):
            @pl.when((c >= src_c) & (c + 1 < nk))
            def _():
                remote(one, one, gz_send.at[w, 1, src_c], gc_recv.at[w], core_peer).wait_send()

            @pl.when((c <= src_c) & (c >= 1))
            def _():
                remote(one, one, gz_send.at[w, 0, src_c], gc_recv.at[w], core_peer).wait_send()

    for h in range(pieces):
        spread(0, c, h, (-1, 1))
    for copy in staged[kb : 2 * kb]:
        copy.wait()
    for h in range(2):
        spread(1, c, h, (-1, 1))
    send_core(0, own).start()

    for copy in staged[2 * kb :]:
        copy.wait()
    for b in range(qb):
        for h in range(H):
            q_h = q_ref[b * BLK : (b + 1) * BLK, h * HD : (h + 1) * HD]
            g_h = g_ref[b * BLK : (b + 1) * BLK, h * HD : (h + 1) * HD]
            qs[b, h * BLK : (h + 1) * BLK, :] = q_h
            gs[b, h * BLK : (h + 1) * BLK, :] = g_h
            qt[b, :, h * BLK : (h + 1) * BLK] = q_h.T
            gt[b, :, h * BLK : (h + 1) * BLK] = g_h.T

    zero_slot = qb * nnz
    kslots[zero_slot] = jnp.zeros((BLK, HD), F32)
    vslots[zero_slot] = jnp.zeros((BLK, HD), F32)
    first_row = (r * nk + c) * qb

    def invert(j, carry):
        for b in range(qb):
            found = jnp.int32(zero_slot)
            for n in range(nnz):
                found = jnp.where(pat_ref[n, first_row + b] == j, b * nnz + n, found)
            inv[b, j] = found
        return carry

    lax.fori_loop(0, key_blocks, invert, 0)
    if nk > 1:
        forward(0, 1)
    for h in range(2, pieces):
        spread(1, c, h, (-1, 1))
    send_core(1, own).start()

    for d in range(2, nk):
        forward(0, d)
        forward(1, d - 1)
    from_y(0, 0, nk - 1)
    if nk > 1:
        forward(1, nk - 1)
    from_y(0, nk - 1, nk)
    from_core(0)

    def partial(w, s, half):
        j = s * kb + half
        value = slots[w][inv[0, j]]
        for b in range(1, qb):
            value = value + slots[w][inv[b, j]]
        return value

    def to_core(w, i, s):
        return remote(outs[w].at[s], core_in.at[w, i], core_send.at[w], core_recv.at[w, i], core_peer)

    def to_y(w, i, s, half, where):
        return remote(
            outs[w].at[s, half], y_in.at[w, i, half], y_send.at[w], y_recv.at[w, i, half], where
        )

    def to_z(w, s, half, where):
        return remote(outs[w].at[s, half], z_in.at[w, c, half], z_send.at[w], z_recv.at[w], where)

    def place(i):
        return far(i % nk), why((i // nk + 1) % ny)

    y_sends = nk * (ny - 1)

    def core_step(w):
        def step(i):
            c_at, y_at = place(i)
            s = shard(c_at, y_at, other)
            for half in range(kb):
                outs[w][s, half] = partial(w, s, half).astype(BF16)
            to_core(w, i, s).start()

        loop(nk * ny, step)

    def y_step(w):
        def step(i):
            c_at, y_at = place(i)
            s = shard(c_at, y_at, core)
            to_core(w, i, s).wait_recv()
            for half in range(kb):
                value = partial(w, s, half) + core_in[w, i, half].astype(F32)
                outs[w][s, half] = value.astype(BF16)
                to_y(w, i, s, half, at(c, y_at, core)).start()

        loop(y_sends, step)

    def summed(w, k, s, half):
        value = partial(w, s, half) + core_in[w, y_sends + k, half].astype(F32)
        for e in range(1, ny):
            value = value + y_in[w, (e - 1) * nk + k, half].astype(F32)
        return value

    def landed(w, k, s, half):
        if half == 0:
            to_core(w, y_sends + k, s).wait_recv()
        for e in range(1, ny):
            to_y(w, (e - 1) * nk + k, s, half, core_peer).wait_recv()

    def z_step(w, k):
        c_at = far(k)
        s = shard(c_at, y, core)
        for half in range(kb):
            landed(w, k, s, half)
            outs[w][s, half] = summed(w, k, s, half).astype(BF16)
            to_z(w, s, half, at(c_at, y, core)).start()

    def finish(w, out):
        for half in range(kb):
            landed(w, nk - 1, own, half)
        if nk > 1:
            some = z_in.at[w, pl.ds(0, nk - 1)]
            remote(some, some, z_send.at[w], z_recv.at[w], core_peer).wait_recv()
        for half in range(kb):
            value = summed(w, nk - 1, own, half)
            for d in range(1, nk):
                value = value + z_in[w, zed(d), half].astype(F32)
            out[half * BLK : (half + 1) * BLK, :] = value.astype(BF16)

    def reduction_sent(w):
        every = outs[w].at[pl.ds(0, nk * ny)]
        remote(every, every, core_send.at[w], z_recv.at[w], core_peer).wait_send()
        if ny > 1:
            part = outs[w].at[pl.ds(0, y_sends)]
            remote(part, part, y_send.at[w], z_recv.at[w], core_peer).wait_send()
        if nk > 1:
            part = outs[w].at[pl.ds(0, nk - 1)]
            remote(part, part, z_send.at[w], z_recv.at[w], core_peer).wait_send()

    def query_results(b):
        attended = att_scr[b]
        grad_q = jnp.zeros((HD, H * BLK), F32)
        for n in range(0, nnz, chunk):
            part = slice(n * BLK, n * BLK + rows)
            grad_q = grad_q + dot_t(kc_scr[b, part, :], ds_scr[b, part, :])
        grad_q = (grad_q * scaling).astype(BF16)
        for h in range(H):
            o_ref[b * BLK : (b + 1) * BLK, h * HD : (h + 1) * HD] = attended[
                :, h * BLK : (h + 1) * BLK
            ].T
            dq_ref[b * BLK : (b + 1) * BLK, h * HD : (h + 1) * HD] = grad_q[
                :, h * BLK : (h + 1) * BLK
            ].T

    for b in range(qb):
        for n in range(nnz):
            j = pat_ref[n, first_row + b]
            kc_scr[b, n * BLK : (n + 1) * BLK, :] = kbuf[j // kb, j % kb]
        top = None
        for n in range(0, nnz, chunk):
            part = slice(n * BLK, n * BLK + rows)
            scores = dot(kc_scr[b, part, :], qt[b])
            s_scr[b, part, :] = scores
            high = jnp.max(scores, axis=0, keepdims=True)
            top = high if top is None else jnp.maximum(top, high)
        total = jnp.zeros((1, H * BLK), F32)
        for n in range(0, nnz, chunk):
            part = slice(n * BLK, n * BLK + rows)
            weights = jnp.exp2((s_scr[b, part, :] - top) * (scaling * math.log2(math.e)))
            s_scr[b, part, :] = weights
            total = total + jnp.sum(weights, axis=0, keepdims=True)
        share = 1.0 / total
        share_scr[b, 0:1, :] = share
        share_scr[b, 1:2, :] = total
        for n in range(0, nnz, chunk):
            part = slice(n * BLK, n * BLK + rows)
            grad_v = dot((s_scr[b, part, :] * share).astype(BF16), gs[b])
            for i in range(chunk):
                vslots[b * nnz + n + i] = grad_v[i * BLK : (i + 1) * BLK]

    if tight:
        gather_sent(0)
    core_step(1)
    from_y(1, 0, nk)
    y_step(1)
    if not tight:
        gather_sent(0)
    from_core(1)

    for b in range(qb):
        for n in range(nnz):
            j = pat_ref[n, first_row + b]
            vc_scr[b, n * BLK : (n + 1) * BLK, :] = vbuf[j // kb, j % kb]
        mix = jnp.zeros((HD, H * BLK), F32)
        for n in range(0, nnz, chunk):
            part = slice(n * BLK, n * BLK + rows)
            mix = mix + dot_t(vc_scr[b, part, :], s_scr[b, part, :].astype(BF16))
        share = share_scr[b, 0:1, :]
        attended = (mix / share_scr[b, 1:2, :]).astype(BF16)
        delta = jnp.sum(gt[b].astype(F32) * attended.astype(F32), axis=0, keepdims=True)
        att_scr[b] = attended
        for n in range(0, nnz, chunk):
            part = slice(n * BLK, n * BLK + rows)
            grad_prob = dot(vc_scr[b, part, :], gt[b])
            prob = s_scr[b, part, :] * share
            grad_score = (prob * (grad_prob - delta)).astype(BF16)
            grad_k = dot(grad_score, qs[b]) * scaling
            ds_scr[b, part, :] = grad_score
            for i in range(chunk):
                kslots[b * nnz + n + i] = grad_k[i * BLK : (i + 1) * BLK]

    if tight:
        gather_sent(1)
    core_step(0)
    if nk > 1:
        z_step(1, 0)
    y_step(0)
    for k in range(1, nk - 1):
        z_step(1, k)
    if not tight:
        gather_sent(1)
    if nk > 1:
        z_step(0, 0)
    finish(1, dv_ref)
    for k in range(1, nk - 1):
        z_step(0, k)
    for b in range(qb):
        query_results(b)
    reduction_sent(1)
    finish(0, dk_ref)
    reduction_sent(0)


def write_out(*refs):
    half = len(refs) // 2
    sem = refs[-1]
    copies = [
        pltpu.make_async_copy(src, dst, sem.at[i])
        for i, (src, dst) in enumerate(zip(refs[:half], refs[half:-1]))
    ]
    for copy in copies:
        copy.start()
    for copy in copies:
        copy.wait()


def to_hbm(results):
    n = len(results)
    return pl.pallas_call(
        write_out,
        out_shape=tuple(jax.ShapeDtypeStruct(a.shape, a.dtype) for a in results),
        in_specs=[pl.BlockSpec(memory_space=pltpu.VMEM)] * n,
        out_specs=(pl.BlockSpec(memory_space=pl.ANY),) * n,
        scratch_shapes=[pltpu.SemaphoreType.DMA((n,))],
        compiler_params=pltpu.CompilerParams(vmem_limit_bytes=4 * 1024 * 1024),
    )(*results)


def body(nq, nk, queries, keys, values, out_grad, pattern):
    pattern = pattern.T
    nnz = pattern.shape[0]
    ny = nq // 2
    qb = queries.shape[0] // BLK
    kb = keys.shape[0] // BLK
    shards = nq * nk
    block = (kb, BLK, HD)
    y_sends = max(nk * (ny - 1), 1)
    dma = pltpu.SemaphoreType.DMA
    vmem = pl.BlockSpec(memory_space=pltpu.VMEM)
    results = pl.pallas_call(
        functools.partial(kernel, nq, nk, nnz),
        out_shape=(
            pltpu.VMEM(queries.shape, BF16),
            pltpu.VMEM(queries.shape, BF16),
            pltpu.VMEM(keys.shape, BF16),
            pltpu.VMEM(keys.shape, BF16),
        ),
        in_specs=[pl.BlockSpec(memory_space=pl.ANY)] * 5,
        out_specs=(vmem,) * 4,
        scratch_shapes=[
            pltpu.VMEM(queries.shape, BF16),
            pltpu.VMEM(queries.shape, BF16),
            pltpu.VMEM((shards,) + block, BF16),
            pltpu.VMEM((shards,) + block, BF16),
            pltpu.VMEM((shards if shards <= 64 else 1,) + block, BF16),
            pltpu.VMEM((2, nk * ny) + block, BF16),
            pltpu.VMEM((2, y_sends) + block, BF16),
            pltpu.VMEM((2, nk) + block, BF16),
            pltpu.VMEM((qb * nnz + 1, BLK, HD), F32),
            pltpu.VMEM((qb * nnz + 1, BLK, HD), F32),
            pltpu.VMEM((qb, nnz * BLK, H * BLK), F32),
            pltpu.VMEM((qb, 8, H * BLK), F32),
            pltpu.VMEM((qb, H * BLK, HD), BF16),
            pltpu.VMEM((qb, H * BLK, HD), BF16),
            pltpu.VMEM((qb, HD, H * BLK), BF16),
            pltpu.VMEM((qb, HD, H * BLK), BF16),
            pltpu.VMEM((qb, nnz * BLK, HD), BF16),
            pltpu.VMEM((qb, nnz * BLK, HD), BF16),
            pltpu.VMEM((qb, HD, H * BLK), BF16),
            pltpu.VMEM((qb, nnz * BLK, H * BLK), BF16),
            pltpu.SMEM(pattern.shape, jnp.int32),
            pltpu.SMEM((qb, shards * kb), jnp.int32),
            dma((2 * kb + 3,)),
            dma((2, 2, nk)),
            dma((2, nk, 2 * kb)),
            dma((2,)),
            dma((2, max(ny - 1, 1), nk)),
            dma((2,)),
            dma((2,)),
            dma((2,)),
            dma((2, nk * ny)),
            dma((2,)),
            dma((2, y_sends, kb)),
            dma((2,)),
            dma((2,)),
        ],
        compiler_params=pltpu.CompilerParams(
            collective_id=0, has_side_effects=True, vmem_limit_bytes=60 * 1024 * 1024
        ),
    )(queries, out_grad, keys, values, pattern)
    return to_hbm(results)


def solution(mesh):
    return jax.shard_map(
        functools.partial(body, mesh.shape["qrow"], mesh.shape["kcol"]),
        mesh=mesh,
        in_specs=(
            P(("groups", "qrow", "kcol"), None),
            P(("groups", "kcol", "qrow"), None),
            P(("groups", "kcol", "qrow"), None),
            P(("groups", "qrow", "kcol"), None),
            P("groups", None),
        ),
        out_specs=(
            P(("groups", "qrow", "kcol"), None),
            P(("groups", "qrow", "kcol"), None),
            P(("groups", "kcol", "qrow"), None),
            P(("groups", "kcol", "qrow"), None),
        ),
        check_vma=False,
    )
```
